256 devices in a mesh: ctx: 8 (over x_hi, y), ep: 32 (over z, x_lo, core).
Axes of the slice: x: 4 (x_hi: 2, x_lo: 2; x = x_hi * 2 + x_lo), y: 4, z: 8, core: 2. Of those that a mesh axis runs over, the one named last changes fastest.
Arguments:
- queries: bfloat16 [32, 1024, 2048], P('ep', 'ctx'), may hold values from -28 to 28
- keys: bfloat16 [32, 1024, 256], P('ep', 'ctx'), may hold values from -6 to 6
- values: bfloat16 [32, 1024, 256], P('ep', 'ctx'), may hold values from -6 to 6
- docs: int32 [32, 1024], P('ep', 'ctx'), may hold values from 0 to 2, as said below
- resid: bfloat16 [32, 1024, 2048], P('ep', 'ctx'), may hold values from -6 to 6
- norm_gain: float32 [2048], replicated, may hold values from 0.25 to 1.75
- routes: int32 [32, 1024, 4], P('ep', 'ctx'), may hold values from 0 to 31, all different within a row; in each aligned block of 128 rows (0 to 127, 128 to 255, ..., all dimensions but the last counted through in order) at most 20 rows name the same one
- gates: float32 [32, 1024, 4], P('ep', 'ctx'), may hold values from 0.1 to 1
- w_gate: bfloat16 [32, 2048, 384], P('ep', 'ctx'), may hold values from -0.125 to 0.125
- w_up: bfloat16 [32, 2048, 384], P('ep', 'ctx'), may hold values from -0.125 to 0.125
- w_down: bfloat16 [32, 2048, 384], P('ep', 'ctx'), may hold values from -0.3125 to 0.3125
- grad_out: bfloat16 [32, 1024, 2048], P('ep', 'ctx'), may hold values from -6 to 6
Outputs:
- block_out: bfloat16 [32, 1024, 2048], P('ep', 'ctx')
- query_grad: bfloat16 [32, 1024, 2048], P('ep', 'ctx')
- key_grad: bfloat16 [32, 1024, 256], P('ep', 'ctx')
- value_grad: bfloat16 [32, 1024, 256], P('ep', 'ctx')
- resid_grad: bfloat16 [32, 1024, 2048], P('ep', 'ctx')
- gate_grad: float32 [32, 1024, 4], P('ep', 'ctx')
- w_gate_grad: bfloat16 [32, 2048, 384], P('ep', 'ctx')
- w_up_grad: bfloat16 [32, 2048, 384], P('ep', 'ctx')
- w_down_grad: bfloat16 [32, 2048, 384], P('ep', 'ctx')
The draws below stay inside these ranges and needn't reach their ends.
Inputs may be any that keep to these rules, and one draw needn't show every extreme that they name: `docs`: each sequence holds exactly three documents, ids 0, 1 and 2, each a run of one or more positions, in this order. `routes`: the 4 entries of a token name different experts. Among the tokens of one device (the aligned blocks of 128 positions of a sequence), no expert is named more than 20 times, a bound that some block reaches.
All inputs are finite; a program needn't handle non-finite values.
Results may differ from the reference program's by a relative error of at most 0.04.
Values may be sent and summed in bfloat16 or wider, within the bound.
A program may use at most 128 MiB of HBM per device.

```python
import math
import jax
import jax.numpy as jnp
import numpy as np
from jax import lax

D = 2048
HQ = 16
HK = 2
HD = 128
FF = 384
TOP = 4
TOK_DEV = 128
SEQ = 1024
SEQS = 32
EXPERTS = 32
CAP = 20
N_CTX = 8
N_EP = 32


def doc_table(key):
    seq_keys = jax.random.split(jax.random.fold_in(key, 11), SEQS)

    def one_row(row_key):
        order = jax.random.permutation(row_key, SEQ - 1) + 1
        bounds = order[:2]
        places = jnp.arange(SEQ)
        return jnp.sum((places[:, None] >= bounds[None, :]).astype(jnp.int32), axis=1)
    return jax.vmap(one_row)(seq_keys)


def draw_docs(key, part):
    return doc_table(key)


def draw_keys(key, part):
    base = jnp.clip(jax.random.normal(jax.random.fold_in(key, 15), (SEQS, SEQ, HK * HD), jnp.float32), -6.0, 6.0)
    return base.astype(jnp.bfloat16)


def draw_queries(key, part):
    base = jnp.clip(jax.random.normal(jax.random.fold_in(key, 16), (SEQS, SEQ, HQ * HD), jnp.float32), -6.0, 6.0)
    return base.astype(jnp.bfloat16)


def steps_of(stream_key, dims, cuts, low, largest):
    def one(axis_at, shards_of):
        heights = jax.random.uniform(jax.random.fold_in(jax.random.fold_in(stream_key, 6), axis_at), (shards_of,), jnp.float32, low / len(cuts), largest / len(cuts))
        return jnp.repeat(jnp.exp(heights), dims[axis_at] // shards_of).reshape((-1,) + (1,) * (len(dims) - axis_at - 1))

    gain = one(*cuts[0])
    for cut in cuts[1:]:
        gain = gain * one(*cut)
    return gain


def assign_block(rng, own, number, rows, count, top, bound, skew):
    sequence = jax.random.permutation(rng, count)
    packed, common = shares(count, rows * top, bound, skew, True), shares(count, rows * top, bound, skew, False)
    places = jnp.arange(count)

    def named(tallies, rotation):
        used = int((tallies > 0).sum())
        fixed = max(1, used // 4)
        shifted = fixed + (places - fixed + rotation * (used - fixed)) % max(1, count - fixed)
        return jnp.zeros((count,), jnp.int32).at[sequence[jnp.where(places < fixed, places, shifted)]].set(jnp.asarray(tallies, jnp.int32))

    tallies = jnp.where(number % 4 == 0, named(packed, number // 4), named(common, number - number // 4 - 1))
    mixed = jax.random.permutation(jax.random.fold_in(own, 3), count)
    source_of, taker = mixed[0:count // 2 * 2:2], mixed[1:count // 2 * 2:2]
    slack = jnp.minimum(tallies[source_of] - 1, bound - tallies[taker]) // 2
    slack = jnp.where((source_of == sequence[0]) | (taker == sequence[0]) | (tallies[taker] == 0), 0, jnp.maximum(slack, 0))
    shifted = jax.random.randint(jax.random.fold_in(own, 4), (count // 2,), 0, 1 << 20) % (slack + 1)
    tallies = tallies.at[source_of].add(-shifted).at[taker].add(shifted)
    items = jnp.searchsorted(jnp.cumsum(tallies), jnp.arange(rows * top), side="right").astype(jnp.int32)
    listing = items.reshape(top, rows).T
    listing = listing[jax.random.permutation(jax.random.fold_in(own, 1), rows)]
    rotation = jax.random.randint(jax.random.fold_in(own, 2), (rows, 1), 0, top)
    return jnp.take_along_axis(listing, (jnp.arange(top)[None, :] + rotation) % top, axis=1)


def shares(amount, total, reach, skew, full):
    weights = [(1 << 20) // math.isqrt(rank ** skew) + 1 for rank in range(1, amount + 1)]
    largest = reach if full else min(reach, max(-(-total // amount), total * weights[0] // sum(weights)))
    least = 1 if total - largest >= amount - 1 else 0
    given, rest = [largest] + [least] * (amount - 1), total - largest - least * (amount - 1)
    while rest > 0:
        movable = [i for i in range(1, amount) if given[i] < largest] or [i for i in range(1, amount) if given[i] < reach]
        pool, left = sum([weights[i] for i in movable]), rest
        for i in movable:
            more = min(reach - given[i], max(1, left * weights[i] // pool), rest)
            given[i] = given[i] + more
            rest = rest - more
    return np.array(given)


def normal_values(own_key, shape, scale, bound, shards=(), held_as=jnp.bfloat16):
    factor_of = steps_of(own_key, shape, shards, -0.22, 0.18) if shards else 1.0
    values = jax.random.normal(own_key, shape, jnp.float32) * scale * factor_of
    return jnp.minimum(jnp.maximum(values, -bound), bound).astype(held_as)


def setup_inputs(seed: int = 0) -> dict:
    arg_keys = jax.random.split(jax.random.key(seed), 13)
    queries = draw_queries(jax.random.fold_in(arg_keys[12], 71), 0)
    keys = draw_keys(jax.random.fold_in(arg_keys[12], 71), 0)
    values = normal_values(arg_keys[2], (SEQS, SEQ, HK * HD), 1.0, 6.0, ((0, 32), (1, 8)))
    docs = draw_docs(jax.random.fold_in(arg_keys[12], 71), 0)
    resid = normal_values(arg_keys[4], (SEQS, SEQ, D), 1.0, 6.0, ((0, 32), (1, 8)))
    norm_gain = jnp.clip(1.0 + 0.15 * jax.random.normal(arg_keys[5], (D,), jnp.float32), 0.25, 1.75)
    routes_keys = jax.random.split(jax.random.fold_in(arg_keys[6], 1), SEQS * SEQ // TOK_DEV)
    routes_turns = jax.random.permutation(jax.random.fold_in(arg_keys[6], 3), SEQS * SEQ // TOK_DEV)
    routes = jax.vmap(lambda own, number: assign_block(jax.random.fold_in(arg_keys[6], 2), own, number, TOK_DEV, EXPERTS, TOP, CAP, 2))(routes_keys, routes_turns).reshape((SEQS, SEQ, TOP))
    gates = jnp.clip(0.1 + 0.9 * jax.random.uniform(arg_keys[7], (SEQS, SEQ, TOP), jnp.float32) ** steps_of(arg_keys[7], (SEQS, SEQ, TOP), ((0, 32), (1, 8)), -0.2, 0.2), 0.1, 1.0)
    w_gate = normal_values(arg_keys[8], (EXPERTS, D, FF), D ** -0.5, 0.125, ((0, 32), (1, 8)))
    w_up = normal_values(arg_keys[9], (EXPERTS, D, FF), D ** -0.5, 0.125, ((0, 32), (1, 8)))
    w_down = normal_values(arg_keys[10], (EXPERTS, D, FF), FF ** -0.5, 0.3125, ((0, 32), (1, 8)))
    grad_out = normal_values(arg_keys[11], (SEQS, SEQ, D), 1.0, 6.0, ((0, 32), (1, 8)))
    return {"queries": queries, "keys": keys, "values": values, "docs": docs, "resid": resid, "norm_gain": norm_gain, "routes": routes, "gates": gates, "w_gate": w_gate, "w_up": w_up, "w_down": w_down, "grad_out": grad_out}


def attention_probs(query_rows, key_rows, doc_row):
    group = HQ // HK
    places = jnp.arange(SEQ)
    grouped = query_rows.astype(jnp.float32).reshape(SEQ, HK, group, HD)
    keyed = key_rows.astype(jnp.float32).reshape(SEQ, HK, HD)
    scores = jnp.einsum('ikgd,jkd->kgij', grouped, keyed) * float(HD) ** (-0.5)
    allowed = (doc_row[:, None] == doc_row[None, :]) & (places[None, :] <= places[:, None])
    masked = jnp.where(allowed, scores, -1e+30)
    highest = lax.optimization_barrier(jnp.max(masked, axis=-1, keepdims=True))
    raised = jnp.where(allowed, jnp.exp(masked - highest), 0.0)
    return raised / lax.optimization_barrier(jnp.sum(raised, axis=-1, keepdims=True))

def attend_forward(items):
    query_rows, key_rows, value_rows, doc_row = items
    probs = attention_probs(query_rows, key_rows, doc_row)
    probs_b = probs.astype(jnp.bfloat16)
    valued = value_rows.astype(jnp.float32).reshape(SEQ, HK, HD)
    mixed = jnp.einsum('kgij,jkd->ikgd', probs_b.astype(jnp.float32), valued)
    return mixed.reshape(SEQ, HQ * HD).astype(jnp.bfloat16)

def attend_backward(items):
    query_rows, key_rows, value_rows, doc_row, attn_rows, upstream = items
    group = HQ // HK
    probs = attention_probs(query_rows, key_rows, doc_row)
    probs_b = probs.astype(jnp.bfloat16).astype(jnp.float32)
    grad_heads = upstream.astype(jnp.float32).reshape(SEQ, HK, group, HD)
    attn_heads = attn_rows.astype(jnp.float32).reshape(SEQ, HK, group, HD)
    delta = jnp.einsum('ikgd,ikgd->kgi', grad_heads, attn_heads)
    valued = value_rows.astype(jnp.float32).reshape(SEQ, HK, HD)
    keyed = key_rows.astype(jnp.float32).reshape(SEQ, HK, HD)
    grouped = query_rows.astype(jnp.float32).reshape(SEQ, HK, group, HD)
    d_probs = jnp.einsum('ikgd,jkd->kgij', grad_heads, valued)
    d_scores = (probs * (d_probs - delta[..., None])).astype(jnp.bfloat16).astype(jnp.float32)
    score_scale = float(HD) ** (-0.5)
    query_grad = (jnp.einsum('kgij,jkd->ikgd', d_scores, keyed) * score_scale).reshape(SEQ, HQ * HD)
    key_grad = (jnp.einsum('kgij,ikgd->jkd', d_scores, grouped) * score_scale).reshape(SEQ, HK * HD)
    value_grad = jnp.einsum('kgij,ikgd->jkd', probs_b, grad_heads).reshape(SEQ, HK * HD)
    return (query_grad.astype(jnp.bfloat16), key_grad.astype(jnp.bfloat16), value_grad.astype(jnp.bfloat16))

def ctx_partials(left_rows, right_rows):
    left_split = left_rows.astype(jnp.float32).reshape(N_CTX, N_EP * CAP, -1)
    right_split = right_rows.astype(jnp.float32).reshape(N_CTX, N_EP * CAP, -1)
    partial_sums = jnp.einsum('crd,crf->cdf', left_split, right_split).astype(jnp.bfloat16)
    partial_sums = lax.optimization_barrier(partial_sums)
    return lax.optimization_barrier(jnp.sum(partial_sums.astype(jnp.float32), axis=0)).astype(jnp.bfloat16)

def reference(queries, keys, values, docs, resid, norm_gain, routes, gates, w_gate, w_up, w_down, grad_out):
    attn = lax.map(attend_forward, (queries, keys, values, docs))
    hidden_in = (resid.astype(jnp.float32) + attn.astype(jnp.float32)).astype(jnp.bfloat16)
    hidden_f = hidden_in.astype(jnp.float32)
    rstd = lax.rsqrt(lax.optimization_barrier(jnp.mean(hidden_f * hidden_f, axis=-1, keepdims=True)) + 1e-06)
    normed = (hidden_f * rstd * norm_gain).astype(jnp.bfloat16)
    total_tok = SEQS * SEQ
    assigned = total_tok * TOP
    route_blocks = routes.reshape(SEQS, N_CTX, TOK_DEV * TOP)
    onehot = (route_blocks[..., None] == jnp.arange(EXPERTS, dtype=jnp.int32)).astype(jnp.int32)
    ranks = jnp.cumsum(onehot, axis=2) - onehot
    slots = lax.optimization_barrier(jnp.sum(ranks * onehot, axis=-1))
    seq_index = jnp.arange(SEQS, dtype=jnp.int32)[:, None, None]
    ctx_index = jnp.arange(N_CTX, dtype=jnp.int32)[None, :, None]
    span = N_CTX * N_EP * CAP
    places = ((route_blocks * N_CTX + ctx_index) * N_EP + seq_index) * CAP + slots
    inverse = jnp.full((EXPERTS * span,), assigned, jnp.int32).at[places.reshape(-1)].set(jnp.arange(assigned, dtype=jnp.int32))
    normed_ext = jnp.concatenate([normed.reshape(total_tok, D), jnp.zeros((1, D), jnp.bfloat16)], axis=0)
    upstream_ext = jnp.concatenate([grad_out.reshape(total_tok, D), jnp.zeros((1, D), jnp.bfloat16)], axis=0)
    gate_ext = jnp.concatenate([gates.reshape(assigned), jnp.zeros((1,), jnp.float32)], axis=0)

    def expert_step(carry, expert):
        moe_acc, normed_acc, gate_acc = carry
        chosen = lax.dynamic_slice_in_dim(inverse, expert * span, span)
        token_ids = chosen // TOP
        rows = normed_ext[token_ids]
        weight_rows = gate_ext[chosen]
        upstream_rows = upstream_ext[token_ids].astype(jnp.float32)
        gate_w = w_gate[expert]
        up_w = w_up[expert]
        down_w = w_down[expert]
        pre_gate = jnp.dot(rows, gate_w, preferred_element_type=jnp.float32)
        pre_up = jnp.dot(rows, up_w, preferred_element_type=jnp.float32)
        sigma = jax.nn.sigmoid(pre_gate)
        silu_val = pre_gate * sigma
        activ = (silu_val * pre_up).astype(jnp.bfloat16)
        expert_out = jnp.dot(activ, down_w.T, preferred_element_type=jnp.float32).astype(jnp.bfloat16)
        moe_acc = moe_acc.at[token_ids].add(weight_rows[:, None] * expert_out.astype(jnp.float32))
        gate_acc = gate_acc.at[chosen].set(lax.optimization_barrier(jnp.sum(upstream_rows * expert_out.astype(jnp.float32), axis=-1)))
        d_out = (weight_rows[:, None] * upstream_rows).astype(jnp.bfloat16)
        d_activ = jnp.dot(d_out, down_w, preferred_element_type=jnp.float32)
        d_gate = (d_activ * pre_up * sigma * (1.0 + pre_gate * (1.0 - sigma))).astype(jnp.bfloat16)
        d_up = (d_activ * silu_val).astype(jnp.bfloat16)
        d_row = (jnp.dot(d_gate, gate_w.T, preferred_element_type=jnp.float32) + jnp.dot(d_up, up_w.T, preferred_element_type=jnp.float32)).astype(jnp.bfloat16)
        normed_acc = normed_acc.at[token_ids].add(d_row.astype(jnp.float32))
        grads = (ctx_partials(rows, d_gate), ctx_partials(rows, d_up), ctx_partials(d_out, activ))
        return ((moe_acc, normed_acc, gate_acc), grads)
    start = (jnp.zeros((total_tok + 1, D), jnp.float32), jnp.zeros((total_tok + 1, D), jnp.float32), jnp.zeros((assigned + 1,), jnp.float32))
    (moe_acc, normed_acc, gate_acc), grads = lax.scan(expert_step, start, jnp.arange(EXPERTS, dtype=jnp.int32))
    w_gate_grad, w_up_grad, w_down_grad = grads
    moe_sum = moe_acc[:total_tok].reshape(SEQS, SEQ, D)
    block_out = (hidden_f + moe_sum).astype(jnp.bfloat16)
    gate_grad = gate_acc[:assigned].reshape(SEQS, SEQ, TOP)
    d_normed = normed_acc[:total_tok].reshape(SEQS, SEQ, D)
    scaled = norm_gain * d_normed
    resid_grad = grad_out.astype(jnp.float32) + rstd * scaled - hidden_f * rstd ** 3 * lax.optimization_barrier(jnp.mean(scaled * hidden_f, axis=-1, keepdims=True))
    resid_grad = resid_grad.astype(jnp.bfloat16)
    query_grad, key_grad, value_grad = lax.map(attend_backward, (queries, keys, values, docs, attn, resid_grad))
    return (block_out, query_grad, key_grad, value_grad, resid_grad, gate_grad, w_gate_grad, w_up_grad, w_down_grad)
```

```python
import functools

import jax
import jax.numpy as jnp
from jax import lax
from jax.experimental import pallas as pl
from jax.experimental.pallas import tpu as pltpu
from jax.sharding import PartitionSpec as P

HD = 128
NQ = 4
MESH = pl.DeviceIdType.MESH
F32 = jnp.float32
BF16 = jnp.bfloat16


def dot_nn(a, b):
    return lax.dot_general(a, b, (((1,), (0,)), ((), ())), preferred_element_type=F32)


def dot_nt(a, b):
    return lax.dot_general(a, b, (((1,), (1,)), ((), ())), preferred_element_type=F32)


def dot_tn(a, b):
    return lax.dot_general(a, b, (((0,), (0,)), ((), ())), preferred_element_type=F32)


def iota(shape, dim):
    return lax.broadcasted_iota(jnp.int32, shape, dim)


def block_kernel(
    dims,
    q_ref, k_ref, v_ref, docs_ref, resid_ref, gain_ref, routes_ref, gates_ref,
    wg_ref, wu_ref, wd_ref, go_ref,
    bo_ref, qg_ref, kg_ref, vg_ref, rg_ref, gg_ref, wgo_ref, wuo_ref, wdo_ref,
    dsend, drecv, nsend, nrecv, dret, eret, sel, grows, stk, acc, code_t, gate_t, vt,
    kfull, vfull, docsend, docall, offs, probs, attn, wgu, wdn, xall, doall, dact, dab, act,
    unst, wsend, wrecv, dk_t, dv_t, kvsend, kvrecv,
    ds_s, ds_r, ns_s, ns_r, dr_s, dr_r, er_s, er_r, kv_s, kv_r, w_s, w_r, wg_s, wg_r, kg_s, kg_r,
):
    tok, width, n_ep, n_ctx, cap, top, ff, heads_kv = dims
    ep = lax.axis_index("ep")
    ctx = lax.axis_index("ctx")
    qw = width // NQ
    slab = NQ * cap
    rows_all = n_ep * cap
    group_slabs = 4
    per = 2 if n_ep % 8 == 0 and n_ep >= 32 else 1
    chunk_slabs = group_slabs * per
    n_chunks = n_ep // chunk_slabs
    chunk_rows = chunk_slabs * cap
    shard = width // n_ctx
    heads = width // HD
    group = heads // heads_kv
    scale = float(HD) ** (-0.5)
    kd = heads_kv * HD

    def ep_of(p):
        half = (p + 1) // 2
        odd = p % 2
        return (ep + odd * half + (1 - odd) * (n_ep - half)) % n_ep

    def ep_back(p):
        half = (p + 1) // 2
        odd = p % 2
        return (ep + (1 - odd) * half + odd * (n_ep - half)) % n_ep

    def ctx_of(p):
        return (ctx + p) % n_ctx

    def loop(lo, hi, body):
        def step(i, c):
            body(i)
            return c

        lax.fori_loop(lo, hi, step, 0)

    def rows(start, size, mult):
        return pl.ds(pl.multiple_of(start, mult), size)

    def remote(src, dst, send, recv, axis, dest):
        return pltpu.make_async_remote_copy(
            src_ref=src, dst_ref=dst, send_sem=send, recv_sem=recv,
            device_id={axis: dest}, device_id_type=MESH,
        )

    def to_expert(buf, land, send, recv, p):
        return remote(
            buf.at[rows(ep_of(p) * slab, slab, 16)], land.at[rows(p * slab, slab, 16)],
            send.at[p], recv.at[p], "ep", ep_of(p),
        )

    def to_source(buf, land, send, recv, p):
        return remote(
            buf.at[rows(p * slab, slab, 16)], land.at[rows(ep * slab, slab, 16)],
            send.at[p], recv.at[p], "ep", ep_back(p),
        )

    def own_slab(buf, land, recv, outward):
        mine = rows(ep * slab, slab, 16)
        first = pl.ds(0, slab)
        if outward:
            return pltpu.make_async_copy(buf.at[mine], land.at[first], recv.at[0])
        return pltpu.make_async_copy(buf.at[first], land.at[mine], recv.at[0])

    def kv_copies(p):
        mine = rows(ctx * tok, tok, 128)
        return (
            remote(k_ref, kfull.at[mine], kv_s.at[0, p], kv_r.at[0, p], "ctx", ctx_of(p)),
            remote(v_ref, vfull.at[mine], kv_s.at[1, p], kv_r.at[1, p], "ctx", ctx_of(p)),
            remote(docsend, docall.at[ctx], kv_s.at[2, p], kv_r.at[2, p], "ctx", ctx_of(p)),
        )

    def w_copies(p):
        mine = rows(ctx * shard, shard, 16)
        return (
            remote(wg_ref, wgu.at[mine, pl.ds(0, ff)], w_s.at[0, p], w_r.at[0, p], "ctx", ctx_of(p)),
            remote(wu_ref, wgu.at[mine, pl.ds(ff, ff)], w_s.at[1, p], w_r.at[1, p], "ctx", ctx_of(p)),
            remote(wd_ref, wdn.at[mine], w_s.at[2, p], w_r.at[2, p], "ctx", ctx_of(p)),
        )

    def wg_copy(p):
        return remote(
            wsend.at[rows(ctx_of(p) * shard, shard, 16)], wrecv.at[p],
            wg_s.at[p], wg_r.at[p], "ctx", ctx_of(p),
        )

    def kg_copy(p):
        return remote(
            kvsend.at[rows(ctx_of(p) * tok, tok, 16)], kvrecv.at[p],
            kg_s.at[p], kg_r.at[p], "ctx", ctx_of(p),
        )

    barrier = pltpu.get_barrier_semaphore()
    loop(1, n_ctx, lambda p: pl.semaphore_signal(
        barrier, inc=1, device_id={"ctx": ctx_of(p)}, device_id_type=MESH))
    loop(1, n_ep, lambda p: pl.semaphore_signal(
        barrier, inc=1, device_id={"ep": ep_of(p)}, device_id_type=MESH))
    doc_row = jnp.broadcast_to(docs_ref[...], (8, tok))
    docsend[...] = doc_row

    lane = iota((tok, 128), 1)
    named = jnp.zeros((tok, 128), F32)
    weight = jnp.zeros((tok, 128), F32)
    for k in range(top):
        hit = routes_ref[:, k : k + 1] == lane
        named = jnp.where(hit, 1.0, named)
        weight = jnp.where(hit, gates_ref[:, k : k + 1], weight)
    lower = jnp.where(iota((tok, tok), 0) > iota((tok, tok), 1), 1.0, 0.0).astype(BF16)
    rank = dot_nn(lower, named.astype(BF16))
    code_t[...] = jnp.where(named > 0.5, rank, -1.0).T
    gate_t[...] = weight.T

    row_of = iota((slab, tok), 0)
    quarter = sum((row_of >= j * cap).astype(jnp.int32) for j in range(1, NQ))
    place = (row_of - quarter * cap).astype(F32)

    def build(e):
        hit = jnp.broadcast_to(code_t[pl.ds(e, 1), :], (slab, tok)) == place
        for j in range(NQ):
            sel[rows(e * slab, slab, 16), j * tok : (j + 1) * tok] = jnp.where(
                hit & (quarter == j), 1.0, 0.0).astype(BF16)

    loop(0, n_ep, build)
    for j in range(NQ):
        stk[j * tok : (j + 1) * tok, :] = go_ref[:, j * qw : (j + 1) * qw]

    big = 8 * slab
    n_big = n_ep * slab // big

    def gather_into(dst):
        def body(g):
            at = rows(g * big, big, 16)
            dst[at, :] = dot_nn(sel[at, :], stk[...]).astype(BF16)

        loop(0, n_big, body)

    gather_into(grows)

    def weighted(e):
        hit = jnp.broadcast_to(code_t[pl.ds(e, 1), :], (slab, tok)) == place
        gate = jnp.sum(jnp.where(hit, gate_t[pl.ds(e, 1), :], 0.0), axis=1, keepdims=True)
        at = rows(e * slab, slab, 16)
        dsend[at, :] = (gate * grows[at, :].astype(F32)).astype(BF16)

    loop(0, n_ep, weighted)
    pl.semaphore_wait(barrier, n_ep + n_ctx - 2)

    def start_kv(p):
        for c in kv_copies(p):
            c.start()

    def start_w(p):
        for c in w_copies(p):
            c.start()

    loop(1, n_ctx, start_kv)
    own_slab(dsend, drecv, ds_r, True).start()
    loop(1, n_ep, lambda p: to_expert(dsend, drecv, ds_s, ds_r, p).start())
    loop(1, n_ctx, start_w)

    kfull[rows(ctx * tok, tok, 128), :] = k_ref[...]
    vfull[rows(ctx * tok, tok, 128), :] = v_ref[...]
    docall[ctx] = docsend[...]
    mine_w = rows(ctx * shard, shard, 16)
    wgu[mine_w, 0:ff] = wg_ref[...]
    wgu[mine_w, ff : 2 * ff] = wu_ref[...]
    wdn[mine_w, :] = wd_ref[...]
    out_row = iota((NQ * group_slabs * cap, NQ * group_slabs * cap), 0)
    in_row = iota((NQ * group_slabs * cap, NQ * group_slabs * cap), 1)
    block = group_slabs * cap
    o_q = sum((out_row >= j * block).astype(jnp.int32) for j in range(1, NQ))
    rest = out_row - o_q * block
    o_s = sum((rest >= j * cap).astype(jnp.int32) for j in range(1, group_slabs))
    from_row = o_s * slab + o_q * cap + (rest - o_s * cap)
    unst[...] = jnp.where(in_row == from_row, 1.0, 0.0).astype(BF16)

    def wait_kv(p):
        for c in kv_copies(p):
            c.wait_recv()

    loop(1, n_ctx, wait_kv)

    doc_col = jnp.broadcast_to(docs_ref[...], (tok, tok)).astype(F32).T
    q_pos = ctx * tok + iota((tok, tok), 0)
    for b in range(n_ctx):
        same = doc_col == docall[b, 0:1, :].astype(F32)
        ok = same & (b * tok + iota((tok, tok), 1) <= q_pos)
        offs[:, b * tok : (b + 1) * tok] = jnp.where(ok, 0.0, -1e30)

    def attend(h):
        cols = rows(h * HD, HD, 128)
        kv_cols = rows((h // group) * HD, HD, 128)
        s = dot_nt(q_ref[:, cols], kfull[:, kv_cols]) * scale + offs[...]
        raised = jnp.exp(s - jnp.max(s, axis=1, keepdims=True))
        p = (raised / jnp.sum(raised, axis=1, keepdims=True)).astype(BF16)
        probs[h] = p
        attn[:, cols] = dot_nn(p, vfull[:, kv_cols]).astype(BF16)

    loop(0, heads, attend)

    part = 32

    def hidden_of(at):
        both = resid_ref[at, :].astype(F32) + attn[at, :].astype(F32)
        hidden = both.astype(BF16).astype(F32)
        rstd = lax.rsqrt(jnp.mean(hidden * hidden, axis=1, keepdims=True) + 1e-06)
        return hidden, rstd

    def norm_part(i):
        hidden, rstd = hidden_of(rows(i * part, part, part))
        normed = (hidden * rstd * gain_ref[...]).astype(BF16)
        for j in range(NQ):
            stk[rows(j * tok + i * part, part, part), :] = normed[:, j * qw : (j + 1) * qw]

    loop(0, tok // part, norm_part)
    gather_into(nsend)
    own_slab(nsend, nrecv, ns_r, True).start()
    loop(1, n_ep, lambda p: to_expert(nsend, nrecv, ns_s, ns_r, p).start())

    def wait_w(p):
        for c in w_copies(p):
            c.wait_recv()

    loop(1, n_ctx, wait_w)

    def unstack(src, dst, base_slab, base_row):
        for g in range(per):
            y = dot_nn(unst[...], src[rows(base_slab * slab + g * NQ * block, NQ * block, 16), :])
            y = y.astype(BF16)
            for j in range(NQ):
                dst[rows(base_row + g * block, block, 16), j * qw : (j + 1) * qw] = (
                    y[j * block : (j + 1) * block, :])

    def restack(value, dst, base_slab):
        for g in range(per):
            piece = value[g * block : (g + 1) * block, :]
            tall = jnp.concatenate([piece[:, j * qw : (j + 1) * qw] for j in range(NQ)], axis=0)
            dst[rows(base_slab * slab + g * NQ * block, NQ * block, 16), :] = (
                dot_nn(unst[...], tall).astype(BF16))

    def wait_chunk(buf, land, send, recv, c):
        def one(i):
            to_expert(buf, land, send, recv, c * chunk_slabs + i).wait_recv()

        loop(0, chunk_slabs, one)

    def d_chunk(c):
        wait_chunk(dsend, drecv, ds_s, ds_r, c)
        unstack(drecv, doall, c * chunk_slabs, c * chunk_rows)
        at = rows(c * chunk_rows, chunk_rows, 16)
        dact[at, :] = dot_nn(doall[at, :], wdn[...])

    loop(0, n_chunks, d_chunk)

    def n_chunk(c):
        wait_chunk(nsend, nrecv, ns_s, ns_r, c)
        unstack(nrecv, xall, c * chunk_slabs, c * chunk_rows)
        at = rows(c * chunk_rows, chunk_rows, 16)
        pre = dot_nn(xall[at, :], wgu[...])
        a, b = pre[:, :ff], pre[:, ff:]
        sigma = jax.nn.sigmoid(a)
        silu = a * sigma
        d_act = dact[at, :]
        act[at, :] = (silu * b).astype(BF16)
        dab[at, 0:ff] = (d_act * b * sigma * (1.0 + a * (1.0 - sigma))).astype(BF16)
        dab[at, ff : 2 * ff] = (d_act * silu).astype(BF16)
        restack(dot_nt(dab[at, :], wgu[...]).astype(BF16), drecv, c * chunk_slabs)

        def send_back(i):
            p = c * chunk_slabs + i

            @pl.when(p > 0)
            def _():
                to_source(drecv, dret, dr_s, dr_r, p).start()

        loop(0, chunk_slabs, send_back)
        restack(dot_nt(act[at, :], wdn[...]).astype(BF16), nrecv, c * chunk_slabs)

    loop(0, n_chunks, n_chunk)
    own_slab(drecv, dret, dr_r, False).start()
    own_slab(nrecv, eret, er_r, False).start()
    loop(1, n_ep, lambda p: to_source(nrecv, eret, er_s, er_r, p).start())

    def w_grad(p):
        j = ctx_of(p)
        cols = rows(j * shard, shard, 128)
        at = rows(j * shard, shard, 16)
        wsend[at, 0 : 2 * ff] = dot_tn(xall[:, cols], dab[...]).astype(BF16)
        wsend[at, 2 * ff : 3 * ff] = dot_tn(doall[:, cols], act[...]).astype(BF16)

        @pl.when(p < n_ctx)
        def _():
            wg_copy(p).start()

    loop(1, n_ctx + 1, w_grad)

    def wait_back(buf, land, send, recv):
        def one(p):
            dst = land.at[rows(ep_of(p) * slab, slab, 16)]
            src = buf.at[rows(p * slab, slab, 16)]
            remote(src, dst, send.at[p], recv.at[p], "ep", ep_back(p)).wait_recv()

        loop(1, n_ep, one)
        own_slab(buf, land, recv, False).wait()

    def combine(land):
        acc[...] = jnp.zeros_like(acc)

        def body(g):
            at = rows(g * big, big, 16)
            acc[...] += dot_tn(sel[at, :], land[at, :])

        loop(0, n_big, body)

    def summed(i):
        return jnp.concatenate(
            [acc[rows(j * tok + i * part, part, part), :] for j in range(NQ)], axis=1)

    wait_back(drecv, dret, dr_s, dr_r)
    combine(dret)

    def resid_part(i):
        at = rows(i * part, part, part)
        hidden, rstd = hidden_of(at)
        scaled = gain_ref[...] * summed(i)
        tilt = jnp.mean(scaled * hidden, axis=1, keepdims=True)
        grad = go_ref[at, :].astype(F32) + rstd * scaled - hidden * (rstd * rstd * rstd) * tilt
        rg_ref[at, :] = grad.astype(BF16)

    loop(0, tok // part, resid_part)

    dk_t[...] = jnp.zeros_like(dk_t)
    dv_t[...] = jnp.zeros_like(dv_t)

    def attend_back(h):
        cols = rows(h * HD, HD, 128)
        g = h // group
        kv_cols = rows(g * HD, HD, 128)
        up = rg_ref[:, cols]
        p = probs[h]
        delta = jnp.sum(up.astype(F32) * attn[:, cols].astype(F32), axis=1, keepdims=True)
        d_p = dot_nt(up, vfull[:, kv_cols])
        d_s = (p.astype(F32) * (d_p - delta)).astype(BF16)
        qg_ref[:, cols] = (dot_nn(d_s, kfull[:, kv_cols]) * scale).astype(BF16)
        dk_t[g] += dot_tn(q_ref[:, cols], d_s)
        dv_t[g] += dot_tn(up, p)

    loop(0, heads, attend_back)
    for g in range(heads_kv):
        kvsend[:, g * HD : (g + 1) * HD] = (dk_t[g] * scale).T.astype(BF16)
        kvsend[:, kd + g * HD : kd + (g + 1) * HD] = dv_t[g].T.astype(BF16)
    loop(1, n_ctx, lambda p: kg_copy(p).start())

    wait_back(nrecv, eret, er_s, er_r)

    def gate_part(e):
        at = rows(e * slab, slab, 16)
        hit = jnp.broadcast_to(code_t[pl.ds(e, 1), :], (slab, tok)) == place
        gate = jnp.sum(jnp.where(hit, gate_t[pl.ds(e, 1), :], 0.0), axis=1, keepdims=True)
        out = eret[at, :].astype(F32)
        along = jnp.sum(out * grows[at, :].astype(F32), axis=1, keepdims=True)
        vt[pl.ds(e, 1), :] = jnp.sum(jnp.where(hit, along, 0.0), axis=0, keepdims=True)
        eret[at, :] = (gate * out).astype(BF16)

    vt[...] = jnp.zeros_like(vt)
    loop(0, n_ep, gate_part)
    by_token = vt[...].T
    gate_grad = jnp.zeros((tok, 128), F32)
    for k in range(top):
        hit = routes_ref[:, k : k + 1] == lane
        value = jnp.sum(jnp.where(hit, by_token, 0.0), axis=1, keepdims=True)
        gate_grad = jnp.where(lane == k, value, gate_grad)
    gg_ref[...] = gate_grad[:, :top]
    combine(eret)

    def out_part(i):
        at = rows(i * part, part, part)
        hidden = (resid_ref[at, :].astype(F32) + attn[at, :].astype(F32)).astype(BF16)
        bo_ref[at, :] = (hidden.astype(F32) + summed(i)).astype(BF16)

    loop(0, tok // part, out_part)

    loop(1, n_ctx, lambda p: wg_copy(p).wait_recv())

    def w_out(i):
        at = rows(i * part, part, part)
        total = wsend[rows(ctx * shard + i * part, part, part), :].astype(F32)
        for p in range(1, n_ctx):
            total = total + wrecv[p, at, :].astype(F32)
        total = total.astype(BF16)
        wgo_ref[at, :] = total[:, 0:ff]
        wuo_ref[at, :] = total[:, ff : 2 * ff]
        wdo_ref[at, :] = total[:, 2 * ff : 3 * ff]

    loop(0, shard // part, w_out)
    loop(1, n_ctx, lambda p: kg_copy(p).wait_recv())
    total = kvsend[rows(ctx * tok, tok, 16), :].astype(F32)
    for p in range(1, n_ctx):
        total = total + kvrecv[p].astype(F32)
    kg_ref[...] = total[:, :kd].astype(BF16)
    vg_ref[...] = total[:, kd:].astype(BF16)

    def ep_done(p):
        to_expert(dsend, drecv, ds_s, ds_r, p).wait_send()
        to_expert(nsend, nrecv, ns_s, ns_r, p).wait_send()
        to_source(drecv, dret, dr_s, dr_r, p).wait_send()
        to_source(nrecv, eret, er_s, er_r, p).wait_send()

    def ctx_done(p):
        for c in kv_copies(p) + w_copies(p):
            c.wait_send()
        wg_copy(p).wait_send()
        kg_copy(p).wait_send()

    loop(1, n_ep, ep_done)
    loop(1, n_ctx, ctx_done)


def per_device(
    queries, keys, values, docs, resid, norm_gain, routes, gates, w_gate, w_up, w_down, grad_out
):
    tok, width = queries.shape[1], queries.shape[2]
    n_ep, n_ctx = lax.axis_size("ep"), lax.axis_size("ctx")
    shard, ff = w_gate.shape[1], w_gate.shape[2]
    top = routes.shape[2]
    heads_kv = keys.shape[2] // HD
    cap = max(2, (5 * tok * top + 4 * n_ep - 1) // (4 * n_ep))
    dims = (tok, width, n_ep, n_ctx, cap, top, ff, heads_kv)
    qw, slab, heads, kd = width // NQ, NQ * cap, width // HD, heads_kv * HD
    total, rows_all, tall = tok * n_ctx, n_ep * cap, n_ep * NQ * cap
    dma = pltpu.SemaphoreType.DMA
    vmem = pl.BlockSpec(memory_space=pltpu.VMEM)
    wide = pltpu.VMEM((tall, qw), BF16)
    outs = pl.pallas_call(
        functools.partial(block_kernel, dims),
        out_shape=(
            jax.ShapeDtypeStruct((tok, width), BF16),
            jax.ShapeDtypeStruct((tok, width), BF16),
            jax.ShapeDtypeStruct((tok, kd), BF16),
            jax.ShapeDtypeStruct((tok, kd), BF16),
            jax.ShapeDtypeStruct((tok, width), BF16),
            jax.ShapeDtypeStruct((tok, top), F32),
            jax.ShapeDtypeStruct((shard, ff), BF16),
            jax.ShapeDtypeStruct((shard, ff), BF16),
            jax.ShapeDtypeStruct((shard, ff), BF16),
        ),
        in_specs=[vmem] * 12,
        out_specs=[vmem] * 9,
        scratch_shapes=[
            wide, wide, wide, wide, wide, wide,
            pltpu.VMEM((tall, NQ * tok), BF16), wide,
            pltpu.VMEM((NQ * tok, qw), BF16), pltpu.VMEM((NQ * tok, qw), F32),
            pltpu.VMEM((128, tok), F32), pltpu.VMEM((128, tok), F32), pltpu.VMEM((128, tok), F32),
            pltpu.VMEM((total, kd), BF16), pltpu.VMEM((total, kd), BF16),
            pltpu.VMEM((8, tok), jnp.int32), pltpu.VMEM((n_ctx, 8, tok), jnp.int32),
            pltpu.VMEM((tok, total), F32), pltpu.VMEM((heads, tok, total), BF16),
            pltpu.VMEM((tok, width), BF16),
            pltpu.VMEM((width, 2 * ff), BF16), pltpu.VMEM((width, ff), BF16),
            pltpu.VMEM((rows_all, width), BF16), pltpu.VMEM((rows_all, width), BF16),
            pltpu.VMEM((rows_all, ff), F32), pltpu.VMEM((rows_all, 2 * ff), BF16),
            pltpu.VMEM((rows_all, ff), BF16),
            pltpu.VMEM((4 * slab, 4 * slab), BF16),
            pltpu.VMEM((width, 3 * ff), BF16), pltpu.VMEM((n_ctx, shard, 3 * ff), BF16),
            pltpu.VMEM((heads_kv, HD, total), F32), pltpu.VMEM((heads_kv, HD, total), F32),
            pltpu.VMEM((total, 2 * kd), BF16), pltpu.VMEM((n_ctx, tok, 2 * kd), BF16),
            dma((n_ep,)), dma((n_ep,)), dma((n_ep,)), dma((n_ep,)),
            dma((n_ep,)), dma((n_ep,)), dma((n_ep,)), dma((n_ep,)),
            dma((3, n_ctx)), dma((3, n_ctx)), dma((3, n_ctx)), dma((3, n_ctx)),
            dma((n_ctx,)), dma((n_ctx,)), dma((n_ctx,)), dma((n_ctx,)),
        ],
        compiler_params=pltpu.CompilerParams(
            collective_id=0, has_side_effects=True, vmem_limit_bytes=67_000_000
        ),
        name="moe_block",
    )(
        queries[0], keys[0], values[0], docs, resid[0], norm_gain[None], routes[0], gates[0],
        w_gate[0], w_up[0], w_down[0], grad_out[0],
    )
    return tuple(o[None] for o in outs)


def solution(mesh):
    three = P("ep", "ctx", None)
    return jax.shard_map(
        per_device,
        mesh=mesh,
        in_specs=(
            three, three, three, P("ep", "ctx"), three, P(), three, three,
            three, three, three, three,
        ),
        out_specs=(three,) * 9,
        check_vma=False,
    )
```

```python
import functools

import jax
import jax.numpy as jnp
from jax import lax
from jax.experimental import pallas as pl
from jax.experimental.pallas import tpu as pltpu
from jax.sharding import PartitionSpec as P

HD = 128
NQ = 4
MESH = pl.DeviceIdType.MESH
F32 = jnp.float32
BF16 = jnp.bfloat16


def dot_nn(a, b):
    return lax.dot_general(a, b, (((1,), (0,)), ((), ())), preferred_element_type=F32)


def dot_nt(a, b):
    return lax.dot_general(a, b, (((1,), (1,)), ((), ())), preferred_element_type=F32)


def dot_tn(a, b):
    return lax.dot_general(a, b, (((0,), (0,)), ((), ())), preferred_element_type=F32)


def iota(shape, dim):
    return lax.broadcasted_iota(jnp.int32, shape, dim)


def block_kernel(
    dims,
    q_ref, k_ref, v_ref, docs_ref, resid_ref, gain_ref, routes_ref, gates_ref,
    wg_ref, wu_ref, wd_ref, go_ref,
    bo_ref, qg_ref, kg_ref, vg_ref, rg_ref, gg_ref, wgo_ref, wuo_ref, wdo_ref,
    dsend, drecv, nsend, nrecv, dret, eret, sel, grows, stk, acc, code_t, gate_t, vt,
    kfull, vfull, docsend, docall, offs, probs, attn, wgu, wdn, xall, doall, dact, dab, act,
    unst, wsend, wrecv, dk_t, dv_t, kvsend, kvrecv,
    ds_s, ds_r, ns_s, ns_r, dr_s, dr_r, er_s, er_r, kv_s, kv_r, w_s, w_r, wg_s, wg_r, kg_s, kg_r,
):
    tok, width, n_ep, n_ctx, cap, top, ff, heads_kv = dims
    ep = lax.axis_index("ep")
    ctx = lax.axis_index("ctx")
    qw = width // NQ
    slab = NQ * cap
    rows_all = n_ep * cap
    group_slabs = 4
    per = 2 if n_ep % 8 == 0 and n_ep >= 32 else 1
    chunk_slabs = group_slabs * per
    n_chunks = n_ep // chunk_slabs
    chunk_rows = chunk_slabs * cap
    shard = width // n_ctx
    heads = width // HD
    group = heads // heads_kv
    scale = float(HD) ** (-0.5)
    kd = heads_kv * HD

    def ep_of(p):
        half = (p + 1) // 2
        odd = p % 2
        return (ep + odd * half + (1 - odd) * (n_ep - half)) % n_ep

    def ep_back(p):
        half = (p + 1) // 2
        odd = p % 2
        return (ep + (1 - odd) * half + odd * (n_ep - half)) % n_ep

    def ctx_of(p):
        return (ctx + p) % n_ctx

    n_y = n_ctx // 2
    half_at, y_at = ctx // n_y, ctx % n_y
    across = (1 - half_at) * n_y + y_at

    def y_of(p):
        return half_at * n_y + (y_at + p) % n_y

    def loop(lo, hi, body):
        def step(i, c):
            body(i)
            return c

        lax.fori_loop(lo, hi, step, 0)

    def rows(start, size, mult):
        return pl.ds(pl.multiple_of(start, mult), size)

    def remote(src, dst, send, recv, axis, dest):
        return pltpu.make_async_remote_copy(
            src_ref=src, dst_ref=dst, send_sem=send, recv_sem=recv,
            device_id={axis: dest}, device_id_type=MESH,
        )

    def to_expert(buf, land, send, recv, p):
        return remote(
            buf.at[rows(ep_of(p) * slab, slab, 16)], land.at[rows(p * slab, slab, 16)],
            send.at[p], recv.at[p], "ep", ep_of(p),
        )

    def to_source(buf, land, send, recv, p):
        return remote(
            buf.at[rows(p * slab, slab, 16)], land.at[rows(ep * slab, slab, 16)],
            send.at[p], recv.at[p], "ep", ep_back(p),
        )

    def own_slab(buf, land, recv, outward):
        mine = rows(ep * slab, slab, 16)
        first = pl.ds(0, slab)
        if outward:
            return pltpu.make_async_copy(buf.at[mine], land.at[first], recv.at[0])
        return pltpu.make_async_copy(buf.at[first], land.at[mine], recv.at[0])

    def kv_copies(p):
        mine = rows(ctx * tok, tok, 128)
        return (
            remote(k_ref, kfull.at[mine], kv_s.at[0, p], kv_r.at[0, p], "ctx", ctx_of(p)),
            remote(v_ref, vfull.at[mine], kv_s.at[1, p], kv_r.at[1, p], "ctx", ctx_of(p)),
            remote(docsend, docall.at[ctx], kv_s.at[2, p], kv_r.at[2, p], "ctx", ctx_of(p)),
        )

    def w_own(slot, dest):
        mine = rows(ctx * shard, shard, 16)
        return (
            remote(wg_ref, wgu.at[mine, pl.ds(0, ff)], w_s.at[0, slot], w_r.at[0, slot], "ctx", dest),
            remote(wu_ref, wgu.at[mine, pl.ds(ff, ff)], w_s.at[1, slot], w_r.at[1, slot], "ctx", dest),
            remote(wd_ref, wdn.at[mine], w_s.at[2, slot], w_r.at[2, slot], "ctx", dest),
        )

    def w_across():
        return w_own(0, across)

    def w_along(p):
        return w_own(p, y_of(p))

    def w_relay(p):
        theirs = rows(across * shard, shard, 16)
        slot = n_y + p
        gu, dn = wgu.at[theirs], wdn.at[theirs]
        return (
            remote(gu, gu, w_s.at[0, slot], w_r.at[0, slot], "ctx", y_of(p)),
            remote(dn, dn, w_s.at[2, slot], w_r.at[2, slot], "ctx", y_of(p)),
        )

    def wg_along(p, half):
        to_row = (half * n_y + (y_at + p) % n_y) * shard
        slot = 2 * p + half
        return remote(
            wsend.at[rows(to_row, shard, 16)], wrecv.at[slot],
            wg_s.at[slot], wg_r.at[slot], "ctx", y_of(p),
        )

    def wg_across():
        return remote(
            wsend.at[rows(across * shard, shard, 16)], wrecv.at[0],
            wg_s.at[0], wg_r.at[0], "ctx", across,
        )

    def kg_copy(p):
        return remote(
            kvsend.at[rows(ctx_of(p) * tok, tok, 16)], kvrecv.at[p],
            kg_s.at[p], kg_r.at[p], "ctx", ctx_of(p),
        )

    barrier = pltpu.get_barrier_semaphore()
    loop(1, n_ctx, lambda p: pl.semaphore_signal(
        barrier, inc=1, device_id={"ctx": ctx_of(p)}, device_id_type=MESH))
    loop(1, n_ep, lambda p: pl.semaphore_signal(
        barrier, inc=1, device_id={"ep": ep_of(p)}, device_id_type=MESH))
    doc_row = jnp.broadcast_to(docs_ref[...], (8, tok))
    docsend[...] = doc_row

    lane = iota((tok, 128), 1)
    named = jnp.zeros((tok, 128), F32)
    weight = jnp.zeros((tok, 128), F32)
    for k in range(top):
        hit = routes_ref[:, k : k + 1] == lane
        named = jnp.where(hit, 1.0, named)
        weight = jnp.where(hit, gates_ref[:, k : k + 1], weight)
    lower = jnp.where(iota((tok, tok), 0) > iota((tok, tok), 1), 1.0, 0.0).astype(BF16)
    rank = dot_nn(lower, named.astype(BF16))
    code_t[...] = jnp.where(named > 0.5, rank, -1.0).T
    gate_t[...] = weight.T

    row_of = iota((slab, tok), 0)
    quarter = sum((row_of >= j * cap).astype(jnp.int32) for j in range(1, NQ))
    place = (row_of - quarter * cap).astype(F32)

    def build(e):
        hit = jnp.broadcast_to(code_t[pl.ds(e, 1), :], (slab, tok)) == place
        for j in range(NQ):
            sel[rows(e * slab, slab, 16), j * tok : (j + 1) * tok] = jnp.where(
                hit & (quarter == j), 1.0, 0.0).astype(BF16)

    loop(0, n_ep, build)
    for j in range(NQ):
        stk[j * tok : (j + 1) * tok, :] = go_ref[:, j * qw : (j + 1) * qw]

    big = min(8, n_ep) * slab
    n_big = n_ep * slab // big

    def gather_into(dst):
        def body(g):
            at = rows(g * big, big, 16)
            dst[at, :] = dot_nn(sel[at, :], stk[...]).astype(BF16)

        loop(0, n_big, body)

    gather_into(grows)

    def weighted(e):
        hit = jnp.broadcast_to(code_t[pl.ds(e, 1), :], (slab, tok)) == place
        gate = jnp.sum(jnp.where(hit, gate_t[pl.ds(e, 1), :], 0.0), axis=1, keepdims=True)
        at = rows(e * slab, slab, 16)
        dsend[at, :] = (gate * grows[at, :].astype(F32)).astype(BF16)

    loop(0, n_ep, weighted)
    pl.semaphore_wait(barrier, n_ep + n_ctx - 2)

    def start_kv(p):
        for c in kv_copies(p):
            c.start()

    def start_all(copies):
        for c in copies:
            c.start()

    loop(1, n_ctx, start_kv)
    own_slab(dsend, drecv, ds_r, True).start()
    loop(1, n_ep, lambda p: to_expert(dsend, drecv, ds_s, ds_r, p).start())
    start_all(w_across())
    loop(1, n_y, lambda p: start_all(w_along(p)))

    kfull[rows(ctx * tok, tok, 128), :] = k_ref[...]
    vfull[rows(ctx * tok, tok, 128), :] = v_ref[...]
    docall[ctx] = docsend[...]
    mine_w = rows(ctx * shard, shard, 16)
    wgu[mine_w, 0:ff] = wg_ref[...]
    wgu[mine_w, ff : 2 * ff] = wu_ref[...]
    wdn[mine_w, :] = wd_ref[...]
    out_row = iota((NQ * group_slabs * cap, NQ * group_slabs * cap), 0)
    in_row = iota((NQ * group_slabs * cap, NQ * group_slabs * cap), 1)
    block = group_slabs * cap
    o_q = sum((out_row >= j * block).astype(jnp.int32) for j in range(1, NQ))
    rest = out_row - o_q * block
    o_s = sum((rest >= j * cap).astype(jnp.int32) for j in range(1, group_slabs))
    from_row = o_s * slab + o_q * cap + (rest - o_s * cap)
    unst[...] = jnp.where(in_row == from_row, 1.0, 0.0).astype(BF16)

    def wait_kv(p):
        for c in kv_copies(p):
            c.wait_recv()

    loop(1, n_ctx, wait_kv)

    doc_col = jnp.broadcast_to(docs_ref[...], (tok, tok)).astype(F32).T
    q_pos = ctx * tok + iota((tok, tok), 0)
    for b in range(n_ctx):
        same = doc_col == docall[b, 0:1, :].astype(F32)
        ok = same & (b * tok + iota((tok, tok), 1) <= q_pos)
        offs[:, b * tok : (b + 1) * tok] = jnp.where(ok, 0.0, -1e30)

    def attend(h):
        cols = rows(h * HD, HD, 128)
        kv_cols = rows((h // group) * HD, HD, 128)
        s = dot_nt(q_ref[:, cols], kfull[:, kv_cols]) * scale + offs[...]
        raised = jnp.exp(s - jnp.max(s, axis=1, keepdims=True))
        p = (raised / jnp.sum(raised, axis=1, keepdims=True)).astype(BF16)
        probs[h] = p
        attn[:, cols] = dot_nn(p, vfull[:, kv_cols]).astype(BF16)

    loop(0, heads // 2, attend)
    for c in w_across():
        c.wait_recv()
    loop(1, n_y, lambda p: start_all(w_relay(p)))
    loop(heads // 2, heads, attend)

    part = 32

    def hidden_of(at):
        both = resid_ref[at, :].astype(F32) + attn[at, :].astype(F32)
        hidden = both.astype(BF16).astype(F32)
        rstd = lax.rsqrt(jnp.mean(hidden * hidden, axis=1, keepdims=True) + 1e-06)
        return hidden, rstd

    def norm_part(i):
        hidden, rstd = hidden_of(rows(i * part, part, part))
        normed = (hidden * rstd * gain_ref[...]).astype(BF16)
        for j in range(NQ):
            stk[rows(j * tok + i * part, part, part), :] = normed[:, j * qw : (j + 1) * qw]

    loop(0, tok // part, norm_part)
    gather_into(nsend)
    own_slab(nsend, nrecv, ns_r, True).start()
    loop(1, n_ep, lambda p: to_expert(nsend, nrecv, ns_s, ns_r, p).start())

    def wait_w(p):
        for c in w_along(p) + w_relay(p):
            c.wait_recv()

    loop(1, n_y, wait_w)

    def unstack(src, dst, base_slab, base_row):
        for g in range(per):
            y = dot_nn(unst[...], src[rows(base_slab * slab + g * NQ * block, NQ * block, 16), :])
            y = y.astype(BF16)
            for j in range(NQ):
                dst[rows(base_row + g * block, block, 16), j * qw : (j + 1) * qw] = (
                    y[j * block : (j + 1) * block, :])

    def restack(value, dst, base_slab):
        for g in range(per):
            piece = value[g * block : (g + 1) * block, :]
            tall = jnp.concatenate([piece[:, j * qw : (j + 1) * qw] for j in range(NQ)], axis=0)
            dst[rows(base_slab * slab + g * NQ * block, NQ * block, 16), :] = (
                dot_nn(unst[...], tall).astype(BF16))

    def wait_chunk(buf, land, send, recv, c):
        def one(i):
            to_expert(buf, land, send, recv, c * chunk_slabs + i).wait_recv()

        loop(0, chunk_slabs, one)

    def d_chunk(c):
        wait_chunk(dsend, drecv, ds_s, ds_r, c)
        unstack(drecv, doall, c * chunk_slabs, c * chunk_rows)
        at = rows(c * chunk_rows, chunk_rows, 16)
        dact[at, :] = dot_nn(doall[at, :], wdn[...])

    loop(0, n_chunks, d_chunk)

    def n_chunk(c):
        wait_chunk(nsend, nrecv, ns_s, ns_r, c)
        unstack(nrecv, xall, c * chunk_slabs, c * chunk_rows)
        at = rows(c * chunk_rows, chunk_rows, 16)
        pre = dot_nn(xall[at, :], wgu[...])
        a, b = pre[:, :ff], pre[:, ff:]
        sigma = jax.nn.sigmoid(a)
        silu = a * sigma
        d_act = dact[at, :]
        act[at, :] = (silu * b).astype(BF16)
        dab[at, 0:ff] = (d_act * b * sigma * (1.0 + a * (1.0 - sigma))).astype(BF16)
        dab[at, ff : 2 * ff] = (d_act * silu).astype(BF16)
        restack(dot_nt(dab[at, :], wgu[...]).astype(BF16), drecv, c * chunk_slabs)

        def send_back(i):
            p = c * chunk_slabs + i

            @pl.when(p > 0)
            def _():
                to_source(drecv, dret, dr_s, dr_r, p).start()

        loop(0, chunk_slabs, send_back)
        restack(dot_nt(act[at, :], wdn[...]).astype(BF16), nrecv, c * chunk_slabs)

    loop(0, n_chunks, n_chunk)
    own_slab(drecv, dret, dr_r, False).start()
    own_slab(nrecv, eret, er_r, False).start()
    loop(1, n_ep, lambda p: to_source(nrecv, eret, er_s, er_r, p).start())

    def w_grad(i):
        p, half = (i + 2) // 2, i % 2
        j = half * n_y + (y_at + p) % n_y
        cols = rows(j * shard, shard, 128)
        at = rows(j * shard, shard, 16)
        wsend[at, 0 : 2 * ff] = dot_tn(xall[:, cols], dab[...]).astype(BF16)
        wsend[at, 2 * ff : 3 * ff] = dot_tn(doall[:, cols], act[...]).astype(BF16)

        @pl.when(p < n_y)
        def _():
            wg_along(p, half).start()

    loop(0, n_ctx, w_grad)

    def wait_back(buf, land, send, recv):
        def one(p):
            dst = land.at[rows(ep_of(p) * slab, slab, 16)]
            src = buf.at[rows(p * slab, slab, 16)]
            remote(src, dst, send.at[p], recv.at[p], "ep", ep_back(p)).wait_recv()

        loop(1, n_ep, one)
        own_slab(buf, land, recv, False).wait()

    def combine(land):
        acc[...] = jnp.zeros_like(acc)

        def body(g):
            at = rows(g * big, big, 16)
            acc[...] += dot_tn(sel[at, :], land[at, :])

        loop(0, n_big, body)

    def summed(i):
        return jnp.concatenate(
            [acc[rows(j * tok + i * part, part, part), :] for j in range(NQ)], axis=1)

    wait_back(drecv, dret, dr_s, dr_r)
    combine(dret)

    def resid_part(i):
        at = rows(i * part, part, part)
        hidden, rstd = hidden_of(at)
        scaled = gain_ref[...] * summed(i)
        tilt = jnp.mean(scaled * hidden, axis=1, keepdims=True)
        grad = go_ref[at, :].astype(F32) + rstd * scaled - hidden * (rstd * rstd * rstd) * tilt
        rg_ref[at, :] = grad.astype(BF16)

    loop(0, tok // part, resid_part)

    dk_t[...] = jnp.zeros_like(dk_t)
    dv_t[...] = jnp.zeros_like(dv_t)

    def attend_back(h):
        cols = rows(h * HD, HD, 128)
        g = h // group
        kv_cols = rows(g * HD, HD, 128)
        up = rg_ref[:, cols]
        p = probs[h]
        delta = jnp.sum(up.astype(F32) * attn[:, cols].astype(F32), axis=1, keepdims=True)
        d_p = dot_nt(up, vfull[:, kv_cols])
        d_s = (p.astype(F32) * (d_p - delta)).astype(BF16)
        qg_ref[:, cols] = (dot_nn(d_s, kfull[:, kv_cols]) * scale).astype(BF16)
        dk_t[g] += dot_tn(q_ref[:, cols], d_s)
        dv_t[g] += dot_tn(up, p)

    loop(0, heads, attend_back)
    for g in range(heads_kv):
        kvsend[:, g * HD : (g + 1) * HD] = (dk_t[g] * scale).T.astype(BF16)
        kvsend[:, kd + g * HD : kd + (g + 1) * HD] = dv_t[g].T.astype(BF16)
    loop(1, n_ctx, lambda p: kg_copy(p).start())

    def wait_wg(p):
        wg_along(p, 0).wait_recv()
        wg_along(p, 1).wait_recv()

    loop(1, n_y, wait_wg)

    def y_sum(row, half, at):
        total = wsend[row, :].astype(F32)
        for p in range(1, n_y):
            total = total + wrecv[2 * p + half, at, :].astype(F32)
        return total

    def w_other(i):
        row = rows(across * shard + i * part, part, part)
        wsend[row, :] = y_sum(row, 1 - half_at, rows(i * part, part, part)).astype(BF16)

    loop(0, shard // part, w_other)
    wg_across().start()

    wait_back(nrecv, eret, er_s, er_r)

    def gate_part(e):
        at = rows(e * slab, slab, 16)
        hit = jnp.broadcast_to(code_t[pl.ds(e, 1), :], (slab, tok)) == place
        gate = jnp.sum(jnp.where(hit, gate_t[pl.ds(e, 1), :], 0.0), axis=1, keepdims=True)
        out = eret[at, :].astype(F32)
        along = jnp.sum(out * grows[at, :].astype(F32), axis=1, keepdims=True)
        vt[pl.ds(e, 1), :] = jnp.sum(jnp.where(hit, along, 0.0), axis=0, keepdims=True)
        eret[at, :] = (gate * out).astype(BF16)

    vt[...] = jnp.zeros_like(vt)
    loop(0, n_ep, gate_part)
    by_token = vt[...].T
    gate_grad = jnp.zeros((tok, 128), F32)
    for k in range(top):
        hit = routes_ref[:, k : k + 1] == lane
        value = jnp.sum(jnp.where(hit, by_token, 0.0), axis=1, keepdims=True)
        gate_grad = jnp.where(lane == k, value, gate_grad)
    gg_ref[...] = gate_grad[:, :top]
    combine(eret)

    def out_part(i):
        at = rows(i * part, part, part)
        hidden = (resid_ref[at, :].astype(F32) + attn[at, :].astype(F32)).astype(BF16)
        bo_ref[at, :] = (hidden.astype(F32) + summed(i)).astype(BF16)

    loop(0, tok // part, out_part)

    wg_across().wait_recv()

    def w_out(i):
        at = rows(i * part, part, part)
        total = y_sum(rows(ctx * shard + i * part, part, part), half_at, at)
        total = (total + wrecv[0, at, :].astype(F32)).astype(BF16)
        wgo_ref[at, :] = total[:, 0:ff]
        wuo_ref[at, :] = total[:, ff : 2 * ff]
        wdo_ref[at, :] = total[:, 2 * ff : 3 * ff]

    loop(0, shard // part, w_out)
    loop(1, n_ctx, lambda p: kg_copy(p).wait_recv())
    total = kvsend[rows(ctx * tok, tok, 16), :].astype(F32)
    for p in range(1, n_ctx):
        total = total + kvrecv[p].astype(F32)
    kg_ref[...] = total[:, :kd].astype(BF16)
    vg_ref[...] = total[:, kd:].astype(BF16)

    def ep_done(p):
        to_expert(dsend, drecv, ds_s, ds_r, p).wait_send()
        to_expert(nsend, nrecv, ns_s, ns_r, p).wait_send()
        to_source(drecv, dret, dr_s, dr_r, p).wait_send()
        to_source(nrecv, eret, er_s, er_r, p).wait_send()

    def ctx_done(p):
        for c in kv_copies(p):
            c.wait_send()
        kg_copy(p).wait_send()

    def y_done(p):
        for c in w_along(p) + w_relay(p):
            c.wait_send()
        wg_along(p, 0).wait_send()
        wg_along(p, 1).wait_send()

    loop(1, n_ep, ep_done)
    loop(1, n_ctx, ctx_done)
    loop(1, n_y, y_done)
    for c in w_across():
        c.wait_send()
    wg_across().wait_send()


def hand_over(*refs):
    half = len(refs) // 2
    for src, dst in zip(refs[:half], refs[half:]):
        dst[...] = src[...]


def per_device(
    queries, keys, values, docs, resid, norm_gain, routes, gates, w_gate, w_up, w_down, grad_out
):
    tok, width = queries.shape[1], queries.shape[2]
    n_ep, n_ctx = lax.axis_size("ep"), lax.axis_size("ctx")
    shard, ff = w_gate.shape[1], w_gate.shape[2]
    top = routes.shape[2]
    heads_kv = keys.shape[2] // HD
    cap = max(2, (5 * tok * top + 4 * n_ep - 1) // (4 * n_ep))
    dims = (tok, width, n_ep, n_ctx, cap, top, ff, heads_kv)
    qw, slab, heads, kd = width // NQ, NQ * cap, width // HD, heads_kv * HD
    total, rows_all, tall = tok * n_ctx, n_ep * cap, n_ep * NQ * cap
    dma = pltpu.SemaphoreType.DMA
    vmem = pl.BlockSpec(memory_space=pltpu.VMEM)
    wide = pltpu.VMEM((tall, qw), BF16)
    outs = pl.pallas_call(
        functools.partial(block_kernel, dims),
        out_shape=(
            jax.ShapeDtypeStruct((tok, width), BF16),
            jax.ShapeDtypeStruct((tok, width), BF16),
            jax.ShapeDtypeStruct((tok, kd), BF16),
            jax.ShapeDtypeStruct((tok, kd), BF16),
            jax.ShapeDtypeStruct((tok, width), BF16),
            jax.ShapeDtypeStruct((tok, top), F32),
            jax.ShapeDtypeStruct((shard, ff), BF16),
            jax.ShapeDtypeStruct((shard, ff), BF16),
            jax.ShapeDtypeStruct((shard, ff), BF16),
        ),
        in_specs=[vmem] * 12,
        out_specs=[vmem] * 9,
        scratch_shapes=[
            wide, wide, wide, wide, wide, wide,
            pltpu.VMEM((tall, NQ * tok), BF16), wide,
            pltpu.VMEM((NQ * tok, qw), BF16), pltpu.VMEM((NQ * tok, qw), F32),
            pltpu.VMEM((128, tok), F32), pltpu.VMEM((128, tok), F32), pltpu.VMEM((128, tok), F32),
            pltpu.VMEM((total, kd), BF16), pltpu.VMEM((total, kd), BF16),
            pltpu.VMEM((8, tok), jnp.int32), pltpu.VMEM((n_ctx, 8, tok), jnp.int32),
            pltpu.VMEM((tok, total), F32), pltpu.VMEM((heads, tok, total), BF16),
            pltpu.VMEM((tok, width), BF16),
            pltpu.VMEM((width, 2 * ff), BF16), pltpu.VMEM((width, ff), BF16),
            pltpu.VMEM((rows_all, width), BF16), pltpu.VMEM((rows_all, width), BF16),
            pltpu.VMEM((rows_all, ff), F32), pltpu.VMEM((rows_all, 2 * ff), BF16),
            pltpu.VMEM((rows_all, ff), BF16),
            pltpu.VMEM((4 * slab, 4 * slab), BF16),
            pltpu.VMEM((width, 3 * ff), BF16), pltpu.VMEM((n_ctx, shard, 3 * ff), BF16),
            pltpu.VMEM((heads_kv, HD, total), F32), pltpu.VMEM((heads_kv, HD, total), F32),
            pltpu.VMEM((total, 2 * kd), BF16), pltpu.VMEM((n_ctx, tok, 2 * kd), BF16),
            dma((n_ep,)), dma((n_ep,)), dma((n_ep,)), dma((n_ep,)),
            dma((n_ep,)), dma((n_ep,)), dma((n_ep,)), dma((n_ep,)),
            dma((3, n_ctx)), dma((3, n_ctx)), dma((3, n_ctx)), dma((3, n_ctx)),
            dma((n_ctx,)), dma((n_ctx,)), dma((n_ctx,)), dma((n_ctx,)),
        ],
        compiler_params=pltpu.CompilerParams(
            collective_id=0, has_side_effects=True, vmem_limit_bytes=67_000_000
        ),
        name="moe_block",
    )(
        queries[0], keys[0], values[0], docs, resid[0], norm_gain[None], routes[0], gates[0],
        w_gate[0], w_up[0], w_down[0], grad_out[0],
    )
    outs = pl.pallas_call(
        hand_over,
        out_shape=tuple(jax.ShapeDtypeStruct(o.shape, o.dtype) for o in outs),
        in_specs=[vmem] * len(outs),
        out_specs=[vmem] * len(outs),
        name="outputs",
    )(*outs)
    return tuple(o[None] for o in outs)


def solution(mesh):
    three = P("ep", "ctx", None)
    return jax.shard_map(
        per_device,
        mesh=mesh,
        in_specs=(
            three, three, three, P("ep", "ctx"), three, P(), three, three,
            three, three, three, three,
        ),
        out_specs=(three,) * 9,
        check_vma=False,
    )
```

```python
import functools

import jax
import jax.numpy as jnp
from jax import lax
from jax.experimental import pallas as pl
from jax.experimental.pallas import tpu as pltpu
from jax.sharding import PartitionSpec as P

HD = 128
PLANE = 4
NQ = 4
MESH = pl.DeviceIdType.MESH
F32 = jnp.float32
BF16 = jnp.bfloat16


def dot_nn(a, b):
    return lax.dot_general(a, b, (((1,), (0,)), ((), ())), preferred_element_type=F32)


def dot_nt(a, b):
    return lax.dot_general(a, b, (((1,), (1,)), ((), ())), preferred_element_type=F32)


def dot_tn(a, b):
    return lax.dot_general(a, b, (((0,), (0,)), ((), ())), preferred_element_type=F32)


def iota(shape, dim):
    return lax.broadcasted_iota(jnp.int32, shape, dim)


def block_kernel(
    dims,
    q_ref, k_ref, v_ref, docs_ref, resid_ref, gain_ref, routes_ref, gates_ref,
    wg_ref, wu_ref, wd_ref, go_ref,
    bo_ref, qg_ref, kg_ref, vg_ref, rg_ref, gg_ref, wgo_ref, wuo_ref, wdo_ref,
    psend, drecv, nrecv, dret, eret, sel, psel, gall, nall, acc, tabs, code_t, gate_t, vt,
    kfull, vfull, docsend, docall, offs, probs, attn, wgu, wdn, xall, doall, dact, dab, act,
    unst, wsend, wrecv, dk_t, dv_t, kvsend, kvrecv,
    zg_s, zg_r, zn_s, zn_r, pd_s, pd_r, pn_s, pn_r, dr_s, dr_r, er_s, er_r, kv_s, kv_r, w_s, w_r, wg_s, wg_r, kg_s, kg_r,
):
    tok, width, n_ep, n_ctx, cap, top, ff, heads_kv = dims
    ep = lax.axis_index("ep")
    ctx = lax.axis_index("ctx")
    qw = width // NQ
    slab = NQ * cap
    rows_all = n_ep * cap
    group_slabs = 4
    per = 2 if n_ep % 8 == 0 and n_ep >= 32 else 1
    chunk_slabs = group_slabs * per
    n_chunks = n_ep // chunk_slabs
    chunk_rows = chunk_slabs * cap
    shard = width // n_ctx
    heads = width // HD
    group = heads // heads_kv
    scale = float(HD) ** (-0.5)
    kd = heads_kv * HD

    n_z = n_ep // PLANE
    z_at, m_at = ep // PLANE, ep % PLANE
    hops = n_z // 2
    tall_tok = NQ * tok

    def away(p):
        half = (p + 1) // 2
        odd = p % 2
        return odd * half + (1 - odd) * (n_z - half)

    def z_of(p):
        return (z_at + away(p)) % n_z

    def z_back(p):
        return (z_at + n_z - away(p)) % n_z

    def ep_of(p):
        return (ep + p) % n_ep

    def ctx_of(p):
        return (ctx + p) % n_ctx

    n_y = n_ctx // 2
    half_at, y_at = ctx // n_y, ctx % n_y
    across = (1 - half_at) * n_y + y_at

    def y_of(p):
        return half_at * n_y + (y_at + p) % n_y

    def loop(lo, hi, body):
        def step(i, c):
            body(i)
            return c

        lax.fori_loop(lo, hi, step, 0)

    def rows(start, size, mult):
        return pl.ds(pl.multiple_of(start, mult), size)

    def remote(src, dst, send, recv, axis, dest):
        return pltpu.make_async_remote_copy(
            src_ref=src, dst_ref=dst, send_sem=send, recv_sem=recv,
            device_id={axis: dest}, device_id_type=MESH,
        )

    def ring(buf, send, recv, step, with_tabs):
        up, down = (z_at + 1) % n_z, (z_at + n_z - 1) % n_z
        up_shard, down_shard = (z_at + n_z - step + 1) % n_z, (z_at + step - 1) % n_z
        last = step == hops
        size = tall_tok // 2 if last else tall_tok
        up_rows = rows(up_shard * tall_tok, size, 16)
        down_rows = rows(down_shard * tall_tok + (tall_tok - size), size, 16)
        copies = [
            remote(buf.at[up_rows], buf.at[up_rows], send.at[0, step], recv.at[0, step],
                   "ep", up * PLANE + m_at),
            remote(buf.at[down_rows], buf.at[down_rows], send.at[1, step], recv.at[1, step],
                   "ep", down * PLANE + m_at),
        ]
        if with_tabs:
            copies.append(remote(tabs.at[up_shard], tabs.at[up_shard], send.at[2, step],
                                 recv.at[2, step], "ep", up * PLANE + m_at))
            if not last:
                copies.append(remote(tabs.at[down_shard], tabs.at[down_shard], send.at[3, step],
                                     recv.at[3, step], "ep", down * PLANE + m_at))
        return copies

    def plane_copy(land, send, recv, p, j):
        at = rows((p * PLANE + j) * slab, slab, 16)
        i = p * PLANE + j
        return remote(psend.at[at], land.at[at], send.at[i], recv.at[i], "ep",
                      z_at * PLANE + (m_at + j) % PLANE)

    def to_source(buf, land, send, recv, i):
        p, j = i // PLANE, i % PLANE
        dest = z_of(p) * PLANE + (m_at + PLANE - j) % PLANE
        return remote(
            buf.at[rows(i * slab, slab, 16)], land.at[rows(ep * slab, slab, 16)],
            send.at[i], recv.at[i], "ep", dest,
        )

    def own_slab(buf, land, recv):
        mine = rows(ep * slab, slab, 16)
        return pltpu.make_async_copy(buf.at[pl.ds(0, slab)], land.at[mine], recv.at[0])

    def kv_copies(p):
        mine = rows(ctx * tok, tok, 128)
        return (
            remote(k_ref, kfull.at[mine], kv_s.at[0, p], kv_r.at[0, p], "ctx", ctx_of(p)),
            remote(v_ref, vfull.at[mine], kv_s.at[1, p], kv_r.at[1, p], "ctx", ctx_of(p)),
            remote(docsend, docall.at[ctx], kv_s.at[2, p], kv_r.at[2, p], "ctx", ctx_of(p)),
        )

    def w_own(slot, dest):
        mine = rows(ctx * shard, shard, 16)
        return (
            remote(wg_ref, wgu.at[mine, pl.ds(0, ff)], w_s.at[0, slot], w_r.at[0, slot], "ctx", dest),
            remote(wu_ref, wgu.at[mine, pl.ds(ff, ff)], w_s.at[1, slot], w_r.at[1, slot], "ctx", dest),
            remote(wd_ref, wdn.at[mine], w_s.at[2, slot], w_r.at[2, slot], "ctx", dest),
        )

    def w_across():
        return w_own(0, across)

    def w_along(p):
        return w_own(p, y_of(p))

    def w_relay(p):
        theirs = rows(across * shard, shard, 16)
        slot = n_y + p
        gu, dn = wgu.at[theirs], wdn.at[theirs]
        return (
            remote(gu, gu, w_s.at[0, slot], w_r.at[0, slot], "ctx", y_of(p)),
            remote(dn, dn, w_s.at[2, slot], w_r.at[2, slot], "ctx", y_of(p)),
        )

    def wg_along(p, half):
        to_row = (half * n_y + (y_at + p) % n_y) * shard
        slot = 2 * p + half
        return remote(
            wsend.at[rows(to_row, shard, 16)], wrecv.at[slot],
            wg_s.at[slot], wg_r.at[slot], "ctx", y_of(p),
        )

    def wg_across():
        return remote(
            wsend.at[rows(across * shard, shard, 16)], wrecv.at[0],
            wg_s.at[0], wg_r.at[0], "ctx", across,
        )

    def kg_copy(p):
        return remote(
            kvsend.at[rows(ctx_of(p) * tok, tok, 16)], kvrecv.at[p],
            kg_s.at[p], kg_r.at[p], "ctx", ctx_of(p),
        )

    barrier = pltpu.get_barrier_semaphore()
    loop(1, n_ctx, lambda p: pl.semaphore_signal(
        barrier, inc=1, device_id={"ctx": ctx_of(p)}, device_id_type=MESH))
    loop(1, n_ep, lambda p: pl.semaphore_signal(
        barrier, inc=1, device_id={"ep": ep_of(p)}, device_id_type=MESH))
    doc_row = jnp.broadcast_to(docs_ref[...], (8, tok))
    docsend[...] = doc_row

    lane = iota((tok, 128), 1)
    named = jnp.zeros((tok, 128), F32)
    weight = jnp.zeros((tok, 128), F32)
    for k in range(top):
        hit = routes_ref[:, k : k + 1] == lane
        named = jnp.where(hit, 1.0, named)
        weight = jnp.where(hit, gates_ref[:, k : k + 1], weight)
    lower = jnp.where(iota((tok, tok), 0) > iota((tok, tok), 1), 1.0, 0.0).astype(BF16)
    rank = dot_nn(lower, named.astype(BF16))
    code_t[...] = jnp.where(named > 0.5, rank, -1.0).T
    gate_t[...] = weight.T
    tabs[z_at, 0] = code_t[0:n_ep, :]
    tabs[z_at, 1] = gate_t[0:n_ep, :]
    own_rows = z_at * tall_tok
    for j in range(NQ):
        gall[rows(own_rows + j * tok, tok, 16), :] = go_ref[:, j * qw : (j + 1) * qw]
    pl.semaphore_wait(barrier, n_ep + n_ctx - 2)

    def start_kv(p):
        for c in kv_copies(p):
            c.start()

    def start_all(copies):
        for c in copies:
            c.start()

    def wait_all(copies):
        for c in copies:
            c.wait_recv()

    def grad_ring(step):
        return ring(gall, zg_s, zg_r, step, True)

    def norm_ring(step):
        return ring(nall, zn_s, zn_r, step, False)

    loop(1, n_ctx, start_kv)
    start_all(grad_ring(1))
    start_all(w_across())
    loop(1, n_y, lambda p: start_all(w_along(p)))

    row_of = iota((slab, tok), 0)
    quarter = sum((row_of >= j * cap).astype(jnp.int32) for j in range(1, NQ))
    place = (row_of - quarter * cap).astype(F32)

    def build(e):
        hit = jnp.broadcast_to(code_t[pl.ds(e, 1), :], (slab, tok)) == place
        for j in range(NQ):
            sel[rows(e * slab, slab, 16), j * tok : (j + 1) * tok] = jnp.where(
                hit & (quarter == j), 1.0, 0.0).astype(BF16)

    loop(0, n_ep, build)
    big = min(8, n_ep) * slab
    n_big = n_ep * slab // big

    def pack(p, buf, land, send, recv, weighted):
        zs = z_of(p)
        gates_of = []
        for j in range(PLANE):
            e = z_at * PLANE + (m_at + j) % PLANE
            hit = jnp.broadcast_to(tabs[zs, 0, pl.ds(e, 1), :], (slab, tok)) == place
            for k in range(NQ):
                psel[j * slab : (j + 1) * slab, k * tok : (k + 1) * tok] = jnp.where(
                    hit & (quarter == k), 1.0, 0.0).astype(BF16)
            if weighted:
                gates_of.append(jnp.sum(
                    jnp.where(hit, tabs[zs, 1, pl.ds(e, 1), :], 0.0), axis=1, keepdims=True))
        y = dot_nn(psel[...], buf[rows(zs * tall_tok, tall_tok, 16), :])
        for j in range(PLANE):
            piece = y[j * slab : (j + 1) * slab, :]
            if weighted:
                piece = piece * gates_of[j]
            to = land if j == 0 else psend
            to[rows((p * PLANE + j) * slab, slab, 16), :] = piece.astype(BF16)
        for j in range(1, PLANE):
            plane_copy(land, send, recv, p, j).start()

    def pack_d(p):
        pack(p, gall, drecv, pd_s, pd_r, True)

    def pack_n(p):
        for j in range(1, PLANE):
            plane_copy(drecv, pd_s, pd_r, p, j).wait_send()
        pack(p, nall, nrecv, pn_s, pn_r, False)

    kfull[rows(ctx * tok, tok, 128), :] = k_ref[...]
    vfull[rows(ctx * tok, tok, 128), :] = v_ref[...]
    docall[ctx] = docsend[...]
    mine_w = rows(ctx * shard, shard, 16)
    wgu[mine_w, 0:ff] = wg_ref[...]
    wgu[mine_w, ff : 2 * ff] = wu_ref[...]
    wdn[mine_w, :] = wd_ref[...]
    out_row = iota((NQ * group_slabs * cap, NQ * group_slabs * cap), 0)
    in_row = iota((NQ * group_slabs * cap, NQ * group_slabs * cap), 1)
    block = group_slabs * cap
    o_q = sum((out_row >= j * block).astype(jnp.int32) for j in range(1, NQ))
    rest = out_row - o_q * block
    o_s = sum((rest >= j * cap).astype(jnp.int32) for j in range(1, group_slabs))
    from_row = o_s * slab + o_q * cap + (rest - o_s * cap)
    unst[...] = jnp.where(in_row == from_row, 1.0, 0.0).astype(BF16)

    def wait_kv(p):
        for c in kv_copies(p):
            c.wait_recv()

    loop(1, n_ctx, wait_kv)

    doc_col = jnp.broadcast_to(docs_ref[...], (tok, tok)).astype(F32).T
    q_pos = ctx * tok + iota((tok, tok), 0)
    for b in range(n_ctx):
        same = doc_col == docall[b, 0:1, :].astype(F32)
        ok = same & (b * tok + iota((tok, tok), 1) <= q_pos)
        offs[:, b * tok : (b + 1) * tok] = jnp.where(ok, 0.0, -1e30)

    def attend(h):
        cols = rows(h * HD, HD, 128)
        kv_cols = rows((h // group) * HD, HD, 128)
        s = dot_nt(q_ref[:, cols], kfull[:, kv_cols]) * scale + offs[...]
        raised = jnp.exp(s - jnp.max(s, axis=1, keepdims=True))
        p = (raised / jnp.sum(raised, axis=1, keepdims=True)).astype(BF16)
        probs[h] = p
        attn[:, cols] = dot_nn(p, vfull[:, kv_cols]).astype(BF16)

    for step in range(1, hops + 1):
        loop(heads * (step - 1) // hops, heads * step // hops, attend)
        if step < hops:
            wait_all(grad_ring(step))
            start_all(grad_ring(step + 1))
        if step == (hops + 1) // 2:
            wait_all(w_across())
            loop(1, n_y, lambda p: start_all(w_relay(p)))

    part = 32

    def hidden_of(at):
        both = resid_ref[at, :].astype(F32) + attn[at, :].astype(F32)
        hidden = both.astype(BF16).astype(F32)
        rstd = lax.rsqrt(jnp.mean(hidden * hidden, axis=1, keepdims=True) + 1e-06)
        return hidden, rstd

    def norm_part(i):
        hidden, rstd = hidden_of(rows(i * part, part, part))
        normed = (hidden * rstd * gain_ref[...]).astype(BF16)
        for j in range(NQ):
            nall[rows(own_rows + j * tok + i * part, part, part), :] = (
                normed[:, j * qw : (j + 1) * qw])

    loop(0, tok // part, norm_part)
    start_all(norm_ring(1))

    def wait_w(p):
        for c in w_along(p) + w_relay(p):
            c.wait_recv()

    def unstack(src, dst, base_slab, base_row):
        for g in range(per):
            y = dot_nn(unst[...], src[rows(base_slab * slab + g * NQ * block, NQ * block, 16), :])
            y = y.astype(BF16)
            for j in range(NQ):
                dst[rows(base_row + g * block, block, 16), j * qw : (j + 1) * qw] = (
                    y[j * block : (j + 1) * block, :])

    def restack(value, dst, base_slab):
        for g in range(per):
            piece = value[g * block : (g + 1) * block, :]
            tall = jnp.concatenate([piece[:, j * qw : (j + 1) * qw] for j in range(NQ)], axis=0)
            dst[rows(base_slab * slab + g * NQ * block, NQ * block, 16), :] = (
                dot_nn(unst[...], tall).astype(BF16))

    def wait_chunk(land, send, recv, c):
        for i in range(per):
            for j in range(1, PLANE):
                plane_copy(land, send, recv, c * per + i, j).wait_recv()

    def d_chunk(c):
        wait_chunk(drecv, pd_s, pd_r, c)
        unstack(drecv, doall, c * chunk_slabs, c * chunk_rows)
        at = rows(c * chunk_rows, chunk_rows, 16)
        dact[at, :] = dot_nn(doall[at, :], wdn[...])

    def n_chunk(c):
        wait_chunk(nrecv, pn_s, pn_r, c)
        unstack(nrecv, xall, c * chunk_slabs, c * chunk_rows)
        at = rows(c * chunk_rows, chunk_rows, 16)
        pre = dot_nn(xall[at, :], wgu[...])
        a, b = pre[:, :ff], pre[:, ff:]
        sigma = jax.nn.sigmoid(a)
        silu = a * sigma
        d_act = dact[at, :]
        act[at, :] = (silu * b).astype(BF16)
        dab[at, 0:ff] = (d_act * b * sigma * (1.0 + a * (1.0 - sigma))).astype(BF16)
        dab[at, ff : 2 * ff] = (d_act * silu).astype(BF16)
        restack(dot_nt(dab[at, :], wgu[...]).astype(BF16), drecv, c * chunk_slabs)

        def send_back(i):
            p = c * chunk_slabs + i

            @pl.when(p > 0)
            def _():
                to_source(drecv, dret, dr_s, dr_r, p).start()

        loop(0, chunk_slabs, send_back)
        restack(dot_nt(act[at, :], wdn[...]).astype(BF16), nrecv, c * chunk_slabs)

    def fill(step):
        if step == 1:
            loop(0, n_z // 2, pack_d)
        if step == 2:
            wait_all(grad_ring(hops))
            loop(n_z // 2, n_z, pack_d)
        if step == 3:
            loop(1, n_y, wait_w)
            loop(0, n_chunks // 2, d_chunk)
        if step == 4:
            loop(n_chunks // 2, n_chunks, d_chunk)
            if hops >= 4:
                loop(0, n_chunks // 2, n_chunk)

    packed = 0
    for step in range(1, max(hops, 4) + 1):
        if step > hops and packed < n_z:
            fill(step)
            continue
        fill(step)
        if hops >= 4:
            wait_all(norm_ring(step))
            if step < hops:
                start_all(norm_ring(step + 1))
            ready = n_z if step == hops else 2 * step + 1
            if step >= 2:
                loop(packed, ready, pack_n)
                packed = ready
    if hops < 4:
        for step in range(1, hops + 1):
            wait_all(norm_ring(step))
            if step < hops:
                start_all(norm_ring(step + 1))
        loop(0, n_z, pack_n)
        loop(0, n_chunks // 2, n_chunk)
    loop(n_chunks // 2, n_chunks, n_chunk)
    own_slab(drecv, dret, dr_r).start()
    own_slab(nrecv, eret, er_r).start()
    loop(1, n_ep, lambda p: to_source(nrecv, eret, er_s, er_r, p).start())

    def w_grad(i):
        p, half = (i + 2) // 2, i % 2
        j = half * n_y + (y_at + p) % n_y
        cols = rows(j * shard, shard, 128)
        at = rows(j * shard, shard, 16)
        wsend[at, 0 : 2 * ff] = dot_tn(xall[:, cols], dab[...]).astype(BF16)
        wsend[at, 2 * ff : 3 * ff] = dot_tn(doall[:, cols], act[...]).astype(BF16)

        @pl.when(p < n_y)
        def _():
            wg_along(p, half).start()

    loop(0, n_ctx, w_grad)

    def wait_back(buf, land, send, recv):
        def one(i):
            p, j = i // PLANE, i % PLANE
            frm = z_back(p) * PLANE + (m_at + j) % PLANE
            dst = land.at[rows(frm * slab, slab, 16)]
            src = buf.at[rows(i * slab, slab, 16)]
            remote(src, dst, send.at[i], recv.at[i], "ep", frm).wait_recv()

        loop(1, n_ep, one)
        own_slab(buf, land, recv).wait()

    def combine(land):
        acc[...] = jnp.zeros_like(acc)

        def body(g):
            at = rows(g * big, big, 16)
            acc[...] += dot_tn(sel[at, :], land[at, :])

        loop(0, n_big, body)

    def summed(i):
        return jnp.concatenate(
            [acc[rows(j * tok + i * part, part, part), :] for j in range(NQ)], axis=1)

    for step in range(1, hops + 1):
        for c in norm_ring(step):
            c.wait_send()

    def take_rows(g):
        at = rows(g * big, big, 16)
        nall[at, :] = dot_nn(sel[at, :], gall[rows(own_rows, tall_tok, 16), :]).astype(BF16)

    loop(0, n_big, take_rows)
    wait_back(drecv, dret, dr_s, dr_r)
    combine(dret)

    def resid_part(i):
        at = rows(i * part, part, part)
        hidden, rstd = hidden_of(at)
        scaled = gain_ref[...] * summed(i)
        tilt = jnp.mean(scaled * hidden, axis=1, keepdims=True)
        grad = go_ref[at, :].astype(F32) + rstd * scaled - hidden * (rstd * rstd * rstd) * tilt
        rg_ref[at, :] = grad.astype(BF16)

    loop(0, tok // part, resid_part)

    dk_t[...] = jnp.zeros_like(dk_t)
    dv_t[...] = jnp.zeros_like(dv_t)

    def attend_back(h):
        cols = rows(h * HD, HD, 128)
        g = h // group
        kv_cols = rows(g * HD, HD, 128)
        up = rg_ref[:, cols]
        p = probs[h]
        delta = jnp.sum(up.astype(F32) * attn[:, cols].astype(F32), axis=1, keepdims=True)
        d_p = dot_nt(up, vfull[:, kv_cols])
        d_s = (p.astype(F32) * (d_p - delta)).astype(BF16)
        qg_ref[:, cols] = (dot_nn(d_s, kfull[:, kv_cols]) * scale).astype(BF16)
        dk_t[g] += dot_tn(q_ref[:, cols], d_s)
        dv_t[g] += dot_tn(up, p)

    loop(0, heads, attend_back)
    for g in range(heads_kv):
        kvsend[:, g * HD : (g + 1) * HD] = (dk_t[g] * scale).T.astype(BF16)
        kvsend[:, kd + g * HD : kd + (g + 1) * HD] = dv_t[g].T.astype(BF16)
    loop(1, n_ctx, lambda p: kg_copy(p).start())

    def wait_wg(p):
        wg_along(p, 0).wait_recv()
        wg_along(p, 1).wait_recv()

    loop(1, n_y, wait_wg)

    def y_sum(row, half, at):
        total = wsend[row, :].astype(F32)
        for p in range(1, n_y):
            total = total + wrecv[2 * p + half, at, :].astype(F32)
        return total

    def w_other(i):
        row = rows(across * shard + i * part, part, part)
        wsend[row, :] = y_sum(row, 1 - half_at, rows(i * part, part, part)).astype(BF16)

    loop(0, shard // part, w_other)
    wg_across().start()

    wait_back(nrecv, eret, er_s, er_r)

    def gate_part(e):
        at = rows(e * slab, slab, 16)
        hit = jnp.broadcast_to(code_t[pl.ds(e, 1), :], (slab, tok)) == place
        gate = jnp.sum(jnp.where(hit, gate_t[pl.ds(e, 1), :], 0.0), axis=1, keepdims=True)
        out = eret[at, :].astype(F32)
        along = jnp.sum(out * nall[at, :].astype(F32), axis=1, keepdims=True)
        vt[pl.ds(e, 1), :] = jnp.sum(jnp.where(hit, along, 0.0), axis=0, keepdims=True)
        eret[at, :] = (gate * out).astype(BF16)

    vt[...] = jnp.zeros_like(vt)
    loop(0, n_ep, gate_part)
    by_token = vt[...].T
    gate_grad = jnp.zeros((tok, 128), F32)
    for k in range(top):
        hit = routes_ref[:, k : k + 1] == lane
        value = jnp.sum(jnp.where(hit, by_token, 0.0), axis=1, keepdims=True)
        gate_grad = jnp.where(lane == k, value, gate_grad)
    gg_ref[...] = gate_grad[:, :top]
    combine(eret)

    def out_part(i):
        at = rows(i * part, part, part)
        hidden = (resid_ref[at, :].astype(F32) + attn[at, :].astype(F32)).astype(BF16)
        bo_ref[at, :] = (hidden.astype(F32) + summed(i)).astype(BF16)

    loop(0, tok // part, out_part)

    wg_across().wait_recv()

    def w_out(i):
        at = rows(i * part, part, part)
        total = y_sum(rows(ctx * shard + i * part, part, part), half_at, at)
        total = (total + wrecv[0, at, :].astype(F32)).astype(BF16)
        wgo_ref[at, :] = total[:, 0:ff]
        wuo_ref[at, :] = total[:, ff : 2 * ff]
        wdo_ref[at, :] = total[:, 2 * ff : 3 * ff]

    loop(0, shard // part, w_out)
    loop(1, n_ctx, lambda p: kg_copy(p).wait_recv())
    total = kvsend[rows(ctx * tok, tok, 16), :].astype(F32)
    for p in range(1, n_ctx):
        total = total + kvrecv[p].astype(F32)
    kg_ref[...] = total[:, :kd].astype(BF16)
    vg_ref[...] = total[:, kd:].astype(BF16)

    def ep_done(i):
        to_source(drecv, dret, dr_s, dr_r, i).wait_send()
        to_source(nrecv, eret, er_s, er_r, i).wait_send()

    def plane_done(p):
        for j in range(1, PLANE):
            plane_copy(nrecv, pn_s, pn_r, p, j).wait_send()

    loop(0, n_z, plane_done)
    for step in range(1, hops + 1):
        for c in grad_ring(step):
            c.wait_send()

    def ctx_done(p):
        for c in kv_copies(p):
            c.wait_send()
        kg_copy(p).wait_send()

    def y_done(p):
        for c in w_along(p) + w_relay(p):
            c.wait_send()
        wg_along(p, 0).wait_send()
        wg_along(p, 1).wait_send()

    loop(1, n_ep, ep_done)
    loop(1, n_ctx, ctx_done)
    loop(1, n_y, y_done)
    for c in w_across():
        c.wait_send()
    wg_across().wait_send()


def hand_over(*refs):
    half = len(refs) // 2
    for src, dst in zip(refs[:half], refs[half:]):
        dst[...] = src[...]


def per_device(
    queries, keys, values, docs, resid, norm_gain, routes, gates, w_gate, w_up, w_down, grad_out
):
    tok, width = queries.shape[1], queries.shape[2]
    n_ep, n_ctx = lax.axis_size("ep"), lax.axis_size("ctx")
    shard, ff = w_gate.shape[1], w_gate.shape[2]
    top = routes.shape[2]
    heads_kv = keys.shape[2] // HD
    cap = max(2, (5 * tok * top + 4 * n_ep - 1) // (4 * n_ep))
    dims = (tok, width, n_ep, n_ctx, cap, top, ff, heads_kv)
    qw, slab, heads, kd = width // NQ, NQ * cap, width // HD, heads_kv * HD
    total, rows_all, tall = tok * n_ctx, n_ep * cap, n_ep * NQ * cap
    dma = pltpu.SemaphoreType.DMA
    n_z = n_ep // PLANE
    ring = n_z // 2 + 1
    vmem = pl.BlockSpec(memory_space=pltpu.VMEM)
    wide = pltpu.VMEM((tall, qw), BF16)
    outs = pl.pallas_call(
        functools.partial(block_kernel, dims),
        out_shape=(
            jax.ShapeDtypeStruct((tok, width), BF16),
            jax.ShapeDtypeStruct((tok, width), BF16),
            jax.ShapeDtypeStruct((tok, kd), BF16),
            jax.ShapeDtypeStruct((tok, kd), BF16),
            jax.ShapeDtypeStruct((tok, width), BF16),
            jax.ShapeDtypeStruct((tok, top), F32),
            jax.ShapeDtypeStruct((shard, ff), BF16),
            jax.ShapeDtypeStruct((shard, ff), BF16),
            jax.ShapeDtypeStruct((shard, ff), BF16),
        ),
        in_specs=[vmem] * 12,
        out_specs=[vmem] * 9,
        scratch_shapes=[
            wide, wide, wide, wide, wide,
            pltpu.VMEM((tall, NQ * tok), BF16), pltpu.VMEM((PLANE * slab, NQ * tok), BF16),
            pltpu.VMEM((n_z * NQ * tok, qw), BF16),
            pltpu.VMEM((max(n_z * NQ * tok, tall), qw), BF16),
            pltpu.VMEM((NQ * tok, qw), F32), pltpu.VMEM((n_z, 2, n_ep, tok), F32),
            pltpu.VMEM((128, tok), F32), pltpu.VMEM((128, tok), F32), pltpu.VMEM((128, tok), F32),
            pltpu.VMEM((total, kd), BF16), pltpu.VMEM((total, kd), BF16),
            pltpu.VMEM((8, tok), jnp.int32), pltpu.VMEM((n_ctx, 8, tok), jnp.int32),
            pltpu.VMEM((tok, total), F32), pltpu.VMEM((heads, tok, total), BF16),
            pltpu.VMEM((tok, width), BF16),
            pltpu.VMEM((width, 2 * ff), BF16), pltpu.VMEM((width, ff), BF16),
            pltpu.VMEM((rows_all, width), BF16), pltpu.VMEM((rows_all, width), BF16),
            pltpu.VMEM((rows_all, ff), F32), pltpu.VMEM((rows_all, 2 * ff), BF16),
            pltpu.VMEM((rows_all, ff), BF16),
            pltpu.VMEM((4 * slab, 4 * slab), BF16),
            pltpu.VMEM((width, 3 * ff), BF16), pltpu.VMEM((n_ctx, shard, 3 * ff), BF16),
            pltpu.VMEM((heads_kv, HD, total), F32), pltpu.VMEM((heads_kv, HD, total), F32),
            pltpu.VMEM((total, 2 * kd), BF16), pltpu.VMEM((n_ctx, tok, 2 * kd), BF16),
            dma((4, ring)), dma((4, ring)), dma((2, ring)), dma((2, ring)),
            dma((n_ep,)), dma((n_ep,)), dma((n_ep,)), dma((n_ep,)),
            dma((n_ep,)), dma((n_ep,)), dma((n_ep,)), dma((n_ep,)),
            dma((3, n_ctx)), dma((3, n_ctx)), dma((3, n_ctx)), dma((3, n_ctx)),
            dma((n_ctx,)), dma((n_ctx,)), dma((n_ctx,)), dma((n_ctx,)),
        ],
        compiler_params=pltpu.CompilerParams(
            collective_id=0, has_side_effects=True, vmem_limit_bytes=67_000_000
        ),
        name="moe_block",
    )(
        queries[0], keys[0], values[0], docs, resid[0], norm_gain[None], routes[0], gates[0],
        w_gate[0], w_up[0], w_down[0], grad_out[0],
    )
    outs = pl.pallas_call(
        hand_over,
        out_shape=tuple(jax.ShapeDtypeStruct(o.shape, o.dtype) for o in outs),
        in_specs=[vmem] * len(outs),
        out_specs=[vmem] * len(outs),
        name="outputs",
    )(*outs)
    return tuple(o[None] for o in outs)


def solution(mesh):
    three = P("ep", "ctx", None)
    return jax.shard_map(
        per_device,
        mesh=mesh,
        in_specs=(
            three, three, three, P("ep", "ctx"), three, P(), three, three,
            three, three, three, three,
        ),
        out_specs=(three,) * 9,
        check_vma=False,
    )
```
